256 devices in a mesh: qrow: 16 (over x_hi, y, core), dbcol: 16 (over z, x_lo).
Axes of the slice: x: 4 (x_hi: 2, x_lo: 2; x = x_hi * 2 + x_lo), y: 4, z: 8, core: 2. Of those that a mesh axis runs over, the one named last changes fastest.
Arguments:
- query_desc: bfloat16 [8192, 1024], P('qrow', 'dbcol'), may hold values from -0.1875 to 0.1875
- base_desc: bfloat16 [4096, 1024], P('dbcol', 'qrow'), may hold values from -6 to 6
- slopes: int32 [5], replicated, may hold values from -3 to 3, as said below
Outputs:
- seq_score: bfloat16 [8192, 4096], P('qrow', 'dbcol')
- best_score: float32 [8192], P('qrow')
The draws below stay inside these ranges and needn't reach their ends.
Inputs may be any that keep to these rules, and one draw needn't show every extreme that they name: `slopes`: 5 distinct values that always include -3 and 3.
All inputs are finite; a program needn't handle non-finite values.
Results may differ from the reference program's by a relative error of at most 0.0041.
Values may be sent and summed in bfloat16 or wider, within the bound.
No kernel may reach another device: no remote copies, remote signals or barrier semaphores. Data moves between devices by JAX's collectives and lax.ppermute only.
A program may use at most 64 MiB of HBM per device.

```python
import math
import jax
import jax.numpy as jnp
from jax import lax

F = 1024
SEQ = 20
WIN = 10
SMAX = 3
NSLOPE = 5
ROWS_UP = 19
REACH = 57
HALO = 62
NQ = 8192
NB = 4096


def draw_slopes(key, part):
    middle = jax.random.permutation(key, jnp.arange(-SMAX + 1, SMAX, dtype=jnp.int32))[:NSLOPE - 2]
    return jnp.concatenate([jnp.array([-SMAX], jnp.int32), middle, jnp.array([SMAX], jnp.int32)])


def block_levels(rng, dims, cuts, smallest, largest):
    level, own = 1.0, jax.random.fold_in(rng, 6)
    for position, shards_of in cuts:
        steps = jnp.exp(jax.random.uniform(jax.random.fold_in(own, position), (shards_of,), jnp.float32, smallest / len(cuts), largest / len(cuts)))
        level = level * jnp.repeat(steps, dims[position] // shards_of).reshape([-1 if axis == position else 1 for axis in range(len(dims))])
    return level


def normal_values(stream_key, extent, scale, bound, split=(), kind=jnp.bfloat16):
    level = block_levels(stream_key, extent, split, -0.22, 0.18) if split else 1.0
    entries = jax.random.normal(stream_key, extent, jnp.float32) * scale * level
    return jnp.minimum(jnp.maximum(entries, -bound), bound).astype(kind)


def setup_inputs(seed: int = 0) -> dict:
    splits = jax.random.split(jax.random.key(seed), 4)
    query_desc = normal_values(splits[0], (NQ, F), F ** -0.5, 0.1875, ((0, 16), (1, 16)))
    base_desc = normal_values(splits[1], (NB, F), 1.0, 6.0, ((0, 16), (1, 16)))
    slopes = draw_slopes(jax.random.fold_in(splits[3], 71), 0)
    return {"query_desc": query_desc, "base_desc": base_desc, "slopes": slopes}


spread_floor = 0.5

def normalize(similar, valid_cols, valid_rows, out_cols):
    half_win = WIN // 2
    weights = valid_cols.astype(jnp.float32)
    masked = similar * weights[None, :]
    window_sum = masked[:, 0:out_cols]
    window_sq = window_sum * window_sum
    counts = weights[0:out_cols]
    for offset in range(1, WIN):
        column = masked[:, offset:offset + out_cols]
        window_sum = window_sum + column
        window_sq = window_sq + column * column
        counts = counts + weights[offset:offset + out_cols]
    counts = jnp.maximum(counts, 1.0)[None, :]
    window_mean = window_sum / counts
    window_var = window_sq / counts - window_mean * window_mean
    spread = jnp.sqrt(jnp.maximum(window_var, 0.0))
    middle = similar[:, half_win:half_win + out_cols]
    normed = (middle - window_mean) / jnp.maximum(spread, spread_floor)
    keep = weights[half_win:half_win + out_cols][None, :] * valid_rows.astype(jnp.float32)[:, None]
    return (normed * keep).astype(jnp.bfloat16)

def sequence_scores(normed, slopes, tile_rows, tile_cols):
    best_sum = None
    for slope_pos in range(NSLOPE):
        slope_now = slopes[slope_pos]
        running = jnp.zeros((tile_rows, tile_cols), jnp.float32)
        for back_step in range(SEQ):
            row_first = jnp.int32(ROWS_UP - back_step)
            col_first = (REACH - slope_now * back_step).astype(jnp.int32)
            window = lax.dynamic_slice(normed, (row_first, col_first), (tile_rows, tile_cols))
            running = running + window.astype(jnp.float32)
        best_sum = running if best_sum is None else jnp.maximum(best_sum, running)
    return best_sum * (1.0 / math.sqrt(SEQ))

def reference(query_desc, base_desc, slopes):
    block_rows = math.gcd(NQ, 512)
    query_padded = jnp.concatenate([jnp.zeros((ROWS_UP, F), jnp.bfloat16), query_desc], 0)
    base_padded = jnp.pad(base_desc, ((HALO, HALO), (0, 0)))
    column_ids = jnp.arange(NB + 2 * HALO, dtype=jnp.int32) - HALO
    valid_cols = (column_ids >= 0) & (column_ids < NB)

    def score_block(block_id):
        first_row = (block_id * block_rows).astype(jnp.int32)
        query_block = lax.dynamic_slice_in_dim(query_padded, first_row, block_rows + ROWS_UP, 0)
        similar = lax.dot_general(query_block, base_padded, (((1,), (1,)), ((), ())), preferred_element_type=jnp.float32)
        row_ids = first_row + jnp.arange(block_rows + ROWS_UP, dtype=jnp.int32) - ROWS_UP
        normed = normalize(similar, valid_cols, row_ids >= 0, NB + 2 * REACH)
        scores = sequence_scores(normed, slopes, block_rows, NB)
        return (scores.astype(jnp.bfloat16), lax.optimization_barrier(jnp.max(scores, axis=1)))
    seq_parts, best_parts = lax.map(score_block, jnp.arange(NQ // block_rows, dtype=jnp.int32))
    return (seq_parts.reshape(NQ, NB), best_parts.reshape(NQ))
```

```python
import math

import jax
import jax.numpy as jnp
from jax import lax
from jax.experimental import pallas as pl
from jax.experimental.pallas import tpu as pltpu
from jax.sharding import PartitionSpec as P

SEQ = 20
SMAX = 3
SIDE = 64
ABOVE = 24
TAIL = 128
UNROLL = 4


def shifted(x, by):
    width = x.shape[1]
    by = by % width
    return pltpu.roll(x, by, axis=1) if by else x


def score_kernel(slopes, q_ref, tail_ref, own_ref, other_ref, out_ref, top_ref, normed, best):
    rows, cols = out_ref.shape
    width = own_ref.shape[-1]
    half = own_ref.shape[0] * own_ref.shape[1]
    parity = lax.rem(lax.axis_index("qrow"), 2)
    first_col = lax.axis_index("dbcol") * cols
    total_cols = lax.axis_size("dbcol") * cols

    own = own_ref[...].reshape(half, width)
    other = other_ref[...].reshape(half, width)

    def product(ref, low, count):
        total = None
        for which, part in ((parity, own), (1 - parity, other)):
            left = ref[:, which, :, low : low + count].reshape(half, count)
            piece = lax.dot_general(
                left, part, (((0,), (0,)), ((), ())), preferred_element_type=jnp.float32
            )
            total = piece if total is None else total + piece
        return total

    normed[0:ABOVE, :] = product(tail_ref, 0, TAIL)[TAIL - ABOVE :, :]
    for low in range(0, rows, 256):
        normed[ABOVE + low : ABOVE + low + 256, :] = product(q_ref, low, 256)

    lane = lax.broadcasted_iota(jnp.int32, (8, width), 1)
    col = first_col + jnp.where(lane < width - SIDE, lane, lane - width)
    keep = jnp.where((col >= 0) & (col < total_cols), 1.0, 0.0)
    low = jnp.maximum(col - 5, 0)
    high = jnp.minimum(col + 5, total_cols)
    inverse = 1.0 / jnp.maximum(high - low, 1).astype(jnp.float32)

    def window(x):
        two = x + shifted(x, 1)
        four = two + shifted(two, 2)
        eight = four + shifted(four, 4)
        return shifted(eight + shifted(two, 8), -4)

    def normalise(base, count):
        for t in range(count):
            at = pl.ds(pl.multiple_of(base + 8 * t, 8), 8)
            x = normed[at, :]
            mean = window(x) * inverse
            var = window(x * x) * inverse - mean * mean
            value = (x - mean) * lax.rsqrt(jnp.maximum(var, 0.25)) * keep
            normed[at, :] = value.astype(jnp.bfloat16).astype(jnp.float32)

    normalise(0, ABOVE // 8)

    @pl.loop(0, rows // (8 * UNROLL))
    def _(block):
        normalise(ABOVE + block * (8 * UNROLL), UNROLL)

    row = lax.broadcasted_iota(jnp.int32, (8, width), 0)

    def lowered(now, before, by):
        return pltpu.roll(jnp.where(row >= 8 - by, before, now), by, axis=0)

    def advance(slope, x, carry):
        x_b, two_b, four_b, eight_b, late1, late2 = carry
        x_r = shifted(x, slope)
        two = x + lowered(x_r, x_b, 1)
        two_r = shifted(two, 2 * slope)
        four = two + lowered(two_r, two_b, 2)
        four_r = shifted(four, 4 * slope)
        eight = four + lowered(four_r, four_b, 4)
        eight_r = shifted(eight, 8 * slope)
        total = eight + eight_b + late2
        return total, (x_r, two_r, four_r, eight_r, shifted(four, 16 * slope), late1)

    def run(slope, first):
        carry = (jnp.zeros((8, width), jnp.float32),) * 6
        for t in range(ABOVE // 8):
            _, carry = advance(slope, normed[8 * t : 8 * t + 8, :], carry)

        def block(index, carry):
            for t in range(UNROLL):
                at = pl.multiple_of((index * UNROLL + t) * 8, 8)
                total, carry = advance(slope, normed[pl.ds(at + ABOVE, 8), :], carry)
                total = total[:, :cols]
                if not first:
                    total = jnp.maximum(total, best[pl.ds(at, 8), :])
                best[pl.ds(at, 8), :] = total
            return carry

        lax.fori_loop(0, rows // (8 * UNROLL), block, carry)

    run(-SMAX, True)
    run(SMAX, False)
    for slope in range(-SMAX + 1, SMAX):
        present = slopes[0] == slope
        for at in range(1, slopes.shape[0]):
            present = present | (slopes[at] == slope)
        pl.when(present)(lambda slope=slope: run(slope, False))

    scale = 1.0 / math.sqrt(SEQ)
    for low in range(0, rows, 128):
        scores = best[low : low + 128, :] * scale
        out_ref[low : low + 128, :] = scores.astype(jnp.bfloat16)
        most = scores[:, :128]
        for at in range(128, cols, 128):
            most = jnp.maximum(most, scores[:, at : at + 128])
        top_ref[:, low : low + 128] = jnp.max(most.T, axis=0, keepdims=True)


def broadcast_to(x, peers):
    return jnp.broadcast_to(x[None], (peers,) + x.shape)


def local(query_desc, base_desc, slopes):
    rows, cols = query_desc.shape[0], base_desc.shape[0]
    across, down = lax.axis_size("dbcol"), lax.axis_size("qrow")
    query = query_desc.T
    base = base_desc.T
    depth = query.shape[0]

    after = lax.ppermute(base[:, :SIDE], "dbcol", [(i + 1, i) for i in range(across - 1)])
    before = lax.ppermute(base[:, cols - SIDE :], "dbcol", [(i, i + 1) for i in range(across - 1)])
    wide = jnp.concatenate([base, after, before], axis=1)

    query_all = lax.all_to_all(broadcast_to(query, across), "dbcol", 0, 0)
    tail = lax.ppermute(
        query_all[:, :, rows - TAIL :], "qrow", [(i, i + 1) for i in range(down - 1)]
    )
    same_core = [[2 * k + core for k in range(down // 2)] for core in range(2)]
    own = lax.all_to_all(
        broadcast_to(wide, down // 2), "qrow", 0, 0, axis_index_groups=same_core
    )
    other = lax.ppermute(own, "qrow", [(i, i ^ 1) for i in range(down)])

    vmem = pl.BlockSpec(memory_space=pltpu.VMEM)
    scores, top = pl.pallas_call(
        score_kernel,
        out_shape=(
            jax.ShapeDtypeStruct((rows, cols), jnp.bfloat16),
            jax.ShapeDtypeStruct((1, rows), jnp.float32),
        ),
        in_specs=[pl.BlockSpec(memory_space=pltpu.SMEM), vmem, vmem, vmem, vmem],
        out_specs=(vmem, vmem),
        scratch_shapes=[
            pltpu.VMEM((rows + ABOVE, cols + 2 * SIDE), jnp.float32),
            pltpu.VMEM((rows, cols), jnp.float32),
        ],
        name="score",
    )(
        slopes,
        query_all.reshape(across // 2, 2, depth, rows),
        tail.reshape(across // 2, 2, depth, TAIL),
        own,
        other,
    )
    tops = lax.all_to_all(broadcast_to(top, across), "dbcol", 0, 0)
    return scores, jnp.max(tops[:, 0], axis=0)


def solution(mesh):
    placed = (P("qrow", "dbcol"), P("dbcol", "qrow"), P())
    return jax.shard_map(
        local,
        mesh=mesh,
        in_specs=placed,
        out_specs=(P("qrow", "dbcol"), P("qrow")),
        check_vma=False,
    )
```

```python
import math

import jax
import jax.numpy as jnp
from jax import lax
from jax.experimental import pallas as pl
from jax.experimental.pallas import tpu as pltpu
from jax.sharding import PartitionSpec as P

SEQ = 20
PART = 5
SIDE = 64
PAD = 8
TAIL = 128
LANES = 128


def score_kernel(
    slopes, q_ref, tail_ref, own_ref, other_ref, out_ref, top_ref,
    similar, sums, squares, copies, part, part_late, half, half_late, best,
):
    rows, cols = out_ref.shape
    width = own_ref.shape[-1]
    depth = own_ref.shape[0] * own_ref.shape[1]
    blocks = rows // LANES
    every = range(blocks + 1)
    parity = lax.rem(lax.axis_index("qrow"), 2)
    first_col = lax.axis_index("dbcol") * cols
    total_cols = lax.axis_size("dbcol") * cols

    def rows_at(start):
        return pl.ds(pl.multiple_of(start, 8), 8)

    def tiles(start, count, unroll, body):
        def step(index, carry):
            body(start + index * 8)
            return carry

        lax.fori_loop(0, count, step, 0, unroll=unroll)

    own = own_ref[...].reshape(depth, width)
    other = other_ref[...].reshape(depth, width)
    for ref, low, count, block in ((q_ref, 0, rows, 0), (tail_ref, 0, TAIL, blocks)):
        total = None
        for which, piece in ((parity, own), (1 - parity, other)):
            right = ref[:, which, :, low : low + count].reshape(depth, count)
            product = lax.dot_general(
                piece, right, (((0,), (0,)), ((), ())), preferred_element_type=jnp.float32
            )
            total = product if total is None else total + product
        for c in range(count // LANES):
            similar[block + c, PAD : PAD + width, :] = total[:, c * LANES : (c + 1) * LANES]

    def five(r):
        for c in every:
            x = [similar[c, pl.ds(r + d, 8), :] for d in range(5)]
            sums[c, rows_at(r), :] = (x[0] + x[1]) + (x[2] + x[3]) + x[4]
            x = [v * v for v in x]
            squares[c, rows_at(r), :] = (x[0] + x[1]) + (x[2] + x[3]) + x[4]

    tiles(0, (width + PAD) // 8, 49, five)

    lane = lax.broadcasted_iota(jnp.int32, (8, LANES), 1)
    sublane = lax.broadcasted_iota(jnp.int32, (8, LANES), 0)

    def rolled(values, by):
        turned = [pltpu.roll(v, by, axis=1) for v in values]
        return [jnp.where(lane < by, turned[c - 1], turned[c]) for c in range(len(values))]

    def normalise(r):
        col = sublane + (first_col + r - PAD - SIDE)
        low = jnp.maximum(col - 5, 0)
        high = jnp.minimum(col + 5, total_cols)
        inverse = 1.0 / jnp.maximum(high - low, 1).astype(jnp.float32)
        keep = jnp.where((col >= 0) & (col < total_cols), 1.0, 0.0)
        values = []
        for c in every:
            mean = (sums[c, pl.ds(r - 5, 8), :] + sums[c, rows_at(r), :]) * inverse
            square = (squares[c, pl.ds(r - 5, 8), :] + squares[c, rows_at(r), :]) * inverse
            var = square - mean * mean
            value = (similar[c, rows_at(r), :] - mean) * lax.rsqrt(jnp.maximum(var, 0.25)) * keep
            values.append(value.astype(jnp.bfloat16).astype(jnp.float32))
        for k in range(PART):
            for c, v in enumerate(rolled(values, k) if k else values):
                copies[k, c, rows_at(r), :] = v

    tiles(PAD, width // 8, 24, normalise)

    first = PAD + SIDE

    def one_slope(at, carry):
        slope = slopes[at]
        down = slope > 0
        start_half = jnp.where(down, first - 32, first)
        start_part = jnp.where(down, first - 48, first)

        def add_part(r):
            values = []
            for c in every:
                x = [copies[k, c, pl.ds(r - slope * k, 8), :] for k in range(PART)]
                values.append((x[0] + x[1]) + (x[2] + x[3]) + x[4])
            for c, v in enumerate(values):
                part[c, rows_at(r), :] = v
            for c, v in enumerate(rolled(values, PART)):
                part_late[c, rows_at(r), :] = v

        def add_half(r):
            values = [
                part[c, rows_at(r), :] + part_late[c, pl.ds(r - slope * PART, 8), :] for c in every
            ]
            for c, v in enumerate(values[:-1]):
                half[c, rows_at(r), :] = v
            for c, v in enumerate(rolled(values, 2 * PART)[:-1]):
                half_late[c, rows_at(r), :] = v

        def finish(r):
            for c in range(blocks):
                total = half[c, rows_at(r), :] + half_late[c, pl.ds(r - slope * 2 * PART, 8), :]
                best[c, rows_at(r - first), :] = jnp.maximum(
                    best[c, rows_at(r - first), :], total
                )

        tiles(start_part, (cols + 48) // 8, 38, add_part)
        tiles(start_half, (cols + 32) // 8, 36, add_half)
        tiles(first, cols // 8, 32, finish)
        return carry

    best[...] = jnp.full(best.shape, -jnp.inf, jnp.float32)
    lax.fori_loop(0, slopes.shape[0], one_slope, 0)

    scale = 1.0 / math.sqrt(SEQ)
    for c in range(blocks):
        scores = best[c] * scale
        out_ref[c * LANES : (c + 1) * LANES, :] = scores.T.astype(jnp.bfloat16)
        top_ref[:, c * LANES : (c + 1) * LANES] = jnp.max(scores, axis=0, keepdims=True)


def broadcast_to(x, peers):
    return jnp.broadcast_to(x[None], (peers,) + x.shape)


def local(query_desc, base_desc, slopes):
    rows, cols = query_desc.shape[0], base_desc.shape[0]
    across, down = lax.axis_size("dbcol"), lax.axis_size("qrow")
    query = query_desc.T
    base = base_desc.T
    depth = query.shape[0]

    after = lax.ppermute(base[:, :SIDE], "dbcol", [(i + 1, i) for i in range(across - 1)])
    before = lax.ppermute(base[:, cols - SIDE :], "dbcol", [(i, i + 1) for i in range(across - 1)])
    wide = jnp.concatenate([before, base, after], axis=1)

    query_all = lax.all_to_all(broadcast_to(query, across), "dbcol", 0, 0)
    tail = lax.ppermute(
        query_all[:, :, rows - TAIL :], "qrow", [(i, i + 1) for i in range(down - 1)]
    )
    same_core = [[2 * k + core for k in range(down // 2)] for core in range(2)]
    own = lax.all_to_all(
        broadcast_to(wide, down // 2), "qrow", 0, 0, axis_index_groups=same_core
    )
    other = lax.ppermute(own, "qrow", [(i, i ^ 1) for i in range(down)])

    def tall(lead):
        return pltpu.VMEM(lead + (cols + 2 * SIDE + 2 * PAD, LANES), jnp.float32)

    vmem = pl.BlockSpec(memory_space=pltpu.VMEM)
    scores, top = pl.pallas_call(
        score_kernel,
        out_shape=(
            jax.ShapeDtypeStruct((rows, cols), jnp.bfloat16),
            jax.ShapeDtypeStruct((1, rows), jnp.float32),
        ),
        in_specs=[pl.BlockSpec(memory_space=pltpu.SMEM), vmem, vmem, vmem, vmem],
        out_specs=(vmem, vmem),
        scratch_shapes=[
            tall((rows // LANES + 1,)),
            tall((rows // LANES + 1,)),
            tall((rows // LANES + 1,)),
            tall((PART, rows // LANES + 1)),
            tall((rows // LANES + 1,)),
            tall((rows // LANES + 1,)),
            tall((rows // LANES,)),
            tall((rows // LANES,)),
            pltpu.VMEM((rows // LANES, cols, LANES), jnp.float32),
        ],
        name="score",
    )(
        slopes,
        query_all.reshape(across // 2, 2, depth, rows),
        tail.reshape(across // 2, 2, depth, TAIL),
        own,
        other,
    )
    tops = lax.all_to_all(broadcast_to(top, across), "dbcol", 0, 0)
    return scores, jnp.max(tops[:, 0], axis=0)


def solution(mesh):
    placed = (P("qrow", "dbcol"), P("dbcol", "qrow"), P())
    return jax.shard_map(
        local,
        mesh=mesh,
        in_specs=placed,
        out_specs=(P("qrow", "dbcol"), P("qrow")),
        check_vma=False,
    )
```

```python
import math

import jax
import jax.numpy as jnp
from jax import lax
from jax.experimental import pallas as pl
from jax.experimental.pallas import tpu as pltpu
from jax.sharding import PartitionSpec as P


SEQ = 20
PART = 5
SIDE = 64
PAD = 8
TAIL = 128
LANES = 128


def score_kernel(
    slopes, q_ref, tail_ref, own_ref, other_ref, out_ref, top_ref,
    similar, sums, squares, copies, part, part_late, half, half_late, best,
):
    rows, cols = out_ref.shape
    width = own_ref.shape[-1]
    features = own_ref.shape[1]
    depth = own_ref.shape[0] * features
    blocks = rows // LANES
    every = range(blocks + 1)
    parity = lax.rem(lax.axis_index("qrow"), 2)
    first_col = lax.axis_index("dbcol") * cols
    total_cols = lax.axis_size("dbcol") * cols

    def rows_at(start):
        return pl.ds(pl.multiple_of(start, 8), 8)

    def tiles(start, count, unroll, body):
        def step(index, carry):
            body(start + index * 8)
            return carry

        lax.fori_loop(0, count, step, 0, unroll=unroll)

    own = own_ref[...].reshape(depth, width)
    other = other_ref[...].reshape(depth, width)
    for ref, low, count, block in ((q_ref, 0, rows, 0), (tail_ref, 0, TAIL, blocks)):
        total = None
        for which, piece in ((parity, own), (1 - parity, other)):
            right = ref[:, which, :features, low : low + count].reshape(depth, count)
            product = lax.dot_general(
                piece, right, (((0,), (0,)), ((), ())), preferred_element_type=jnp.float32
            )
            total = product if total is None else total + product
        for c in range(count // LANES):
            similar[block + c, PAD : PAD + width, :] = total[:, c * LANES : (c + 1) * LANES]

    def five(r):
        for c in every:
            x = [similar[c, pl.ds(r + d, 8), :] for d in range(5)]
            sums[c, rows_at(r), :] = (x[0] + x[1]) + (x[2] + x[3]) + x[4]
            x = [v * v for v in x]
            squares[c, rows_at(r), :] = (x[0] + x[1]) + (x[2] + x[3]) + x[4]

    tiles(0, (width + PAD) // 8, 49, five)

    lane = lax.broadcasted_iota(jnp.int32, (8, LANES), 1)
    sublane = lax.broadcasted_iota(jnp.int32, (8, LANES), 0)

    def rolled(values, by):
        turned = [pltpu.roll(v, by, axis=1) for v in values]
        return [jnp.where(lane < by, turned[c - 1], turned[c]) for c in range(len(values))]

    def normalise(r):
        col = sublane + (first_col + r - PAD - SIDE)
        low = jnp.maximum(col - 5, 0)
        high = jnp.minimum(col + 5, total_cols)
        inverse = 1.0 / jnp.maximum(high - low, 1).astype(jnp.float32)
        keep = jnp.where((col >= 0) & (col < total_cols), 1.0, 0.0)
        values = []
        for c in every:
            mean = (sums[c, pl.ds(r - 5, 8), :] + sums[c, rows_at(r), :]) * inverse
            square = (squares[c, pl.ds(r - 5, 8), :] + squares[c, rows_at(r), :]) * inverse
            var = square - mean * mean
            value = (similar[c, rows_at(r), :] - mean) * lax.rsqrt(jnp.maximum(var, 0.25)) * keep
            values.append(value.astype(jnp.bfloat16).astype(jnp.float32))
        for k in range(PART):
            for c, v in enumerate(rolled(values, k) if k else values):
                copies[k, c, rows_at(r), :] = v

    tiles(PAD, width // 8, 24, normalise)

    first = PAD + SIDE

    def one_slope(at, carry):
        slope = slopes[at]
        down = slope > 0
        start_half = jnp.where(down, first - 32, first)
        start_part = jnp.where(down, first - 48, first)

        def add_part(r):
            values = []
            for c in every:
                x = [copies[k, c, pl.ds(r - slope * k, 8), :] for k in range(PART)]
                values.append((x[0] + x[1]) + (x[2] + x[3]) + x[4])
            for c, v in enumerate(values):
                part[c, rows_at(r), :] = v
            for c, v in enumerate(rolled(values, PART)):
                part_late[c, rows_at(r), :] = v

        def add_half(r):
            values = [
                part[c, rows_at(r), :] + part_late[c, pl.ds(r - slope * PART, 8), :] for c in every
            ]
            for c, v in enumerate(values[:-1]):
                half[c, rows_at(r), :] = v
            for c, v in enumerate(rolled(values, 2 * PART)[:-1]):
                half_late[c, rows_at(r), :] = v

        def finish(r):
            for c in range(blocks):
                total = half[c, rows_at(r), :] + half_late[c, pl.ds(r - slope * 2 * PART, 8), :]
                best[c, rows_at(r - first), :] = jnp.maximum(
                    best[c, rows_at(r - first), :], total
                )

        tiles(start_part, (cols + 48) // 8, 38, add_part)
        tiles(start_half, (cols + 32) // 8, 36, add_half)
        tiles(first, cols // 8, 32, finish)
        return carry

    best[...] = jnp.full(best.shape, -jnp.inf, jnp.float32)
    lax.fori_loop(0, slopes.shape[0], one_slope, 0)

    scale = 1.0 / math.sqrt(SEQ)
    for c in range(blocks):
        scores = best[c] * scale
        out_ref[c * LANES : (c + 1) * LANES, :] = scores.T.astype(jnp.bfloat16)
        top_ref[:, c * LANES : (c + 1) * LANES] = jnp.max(scores, axis=0, keepdims=True)


def pack_kernel(query_ref, base_ref, out_ref):
    features, cols = base_ref.shape
    here = lax.axis_index("dbcol")
    base = base_ref[...].astype(jnp.float32)

    def packed(low):
        pieces = [base[at : at + 8, low : low + SIDE] for at in range(0, features, 8)]
        return jnp.concatenate(pieces, axis=1).astype(jnp.bfloat16)

    low, high = packed(0), packed(cols - SIDE)
    query = query_ref[...]
    for peer in range(out_ref.shape[0]):
        out_ref[peer, :features, :] = query
        out_ref[peer, features:, :] = jnp.where(peer > here, high, low)


def widen_kernel(all_ref, base_ref, out_ref, edges, sems):
    features, _ = base_ref.shape
    here = lax.axis_index("dbcol")
    last = lax.axis_size("dbcol") - 1
    copies = []
    for at, peer in enumerate((jnp.maximum(here - 1, 0), jnp.minimum(here + 1, last))):
        source = all_ref.at[peer, pl.ds(features, 8), :]
        copies.append(pltpu.make_async_copy(source, edges.at[at], sems.at[at]))
        copies[-1].start()
    for copy in copies:
        copy.wait()

    def unpacked(at, inside):
        edge = jnp.where(inside, edges[at].astype(jnp.float32), 0.0)
        pieces = [edge[:, low : low + SIDE] for low in range(0, edge.shape[1], SIDE)]
        return jnp.concatenate(pieces, axis=0)

    base = base_ref[...].astype(jnp.float32)
    wide = [unpacked(0, here > 0), base, unpacked(1, here < last)]
    wide = jnp.concatenate(wide, axis=1).astype(jnp.bfloat16)
    for peer in range(out_ref.shape[0]):
        out_ref[peer] = wide


def broadcast_to(x, peers):
    return jnp.broadcast_to(x[None], (peers,) + x.shape)


def whole(query_desc, base_desc, slopes):
    rows, cols = query_desc.shape[0], base_desc.shape[0]
    across, down = lax.axis_size("dbcol"), lax.axis_size("qrow")
    query = query_desc.T
    base = base_desc.T
    depth = query.shape[0]

    vmem = pl.BlockSpec(memory_space=pltpu.VMEM)
    blocks = pl.pallas_call(
        pack_kernel,
        out_shape=jax.ShapeDtypeStruct((across, depth + 8, rows), jnp.bfloat16),
        in_specs=[vmem, vmem],
        out_specs=vmem,
        name="pack",
    )(query, base)
    query_all = lax.all_to_all(blocks, "dbcol", 0, 0)
    tail = lax.ppermute(
        query_all[:, :depth, rows - TAIL :], "qrow", [(i, i + 1) for i in range(down - 1)]
    )
    wide = pl.pallas_call(
        widen_kernel,
        out_shape=jax.ShapeDtypeStruct((down // 2, depth, cols + 2 * SIDE), jnp.bfloat16),
        in_specs=[pl.BlockSpec(memory_space=pl.ANY), vmem],
        out_specs=vmem,
        scratch_shapes=[
            pltpu.VMEM((2, 8, rows), jnp.bfloat16),
            pltpu.SemaphoreType.DMA((2,)),
        ],
        name="widen",
    )(query_all, base)
    same_core = [[2 * k + core for k in range(down // 2)] for core in range(2)]
    own = lax.all_to_all(wide, "qrow", 0, 0, axis_index_groups=same_core)
    other = lax.ppermute(own, "qrow", [(i, i ^ 1) for i in range(down)])

    def tall(lead):
        return pltpu.VMEM(lead + (cols + 2 * SIDE + 2 * PAD, LANES), jnp.float32)

    scores, top = pl.pallas_call(
        score_kernel,
        out_shape=(
            jax.ShapeDtypeStruct((rows, cols), jnp.bfloat16),
            jax.ShapeDtypeStruct((1, rows), jnp.float32),
        ),
        in_specs=[pl.BlockSpec(memory_space=pltpu.SMEM), vmem, vmem, vmem, vmem],
        out_specs=(vmem, vmem),
        scratch_shapes=[
            tall((rows // LANES + 1,)),
            tall((rows // LANES + 1,)),
            tall((rows // LANES + 1,)),
            tall((PART, rows // LANES + 1)),
            tall((rows // LANES + 1,)),
            tall((rows // LANES + 1,)),
            tall((rows // LANES,)),
            tall((rows // LANES,)),
            pltpu.VMEM((rows // LANES, cols, LANES), jnp.float32),
        ],
        name="score",
    )(
        slopes,
        query_all.reshape(across // 2, 2, depth + 8, rows),
        tail.reshape(across // 2, 2, depth, TAIL),
        own,
        other,
    )
    tops = lax.all_to_all(broadcast_to(top, across), "dbcol", 0, 0)
    return scores, jnp.max(tops[:, 0], axis=0)


def solution(mesh):
    placed = (P("qrow", "dbcol"), P("dbcol", "qrow"), P())
    return jax.shard_map(
        whole,
        mesh=mesh,
        in_specs=placed,
        out_specs=(P("qrow", "dbcol"), P("qrow")),
        check_vma=False,
    )
```

```python
import math

import jax
import jax.numpy as jnp
from jax import lax
from jax.experimental import pallas as pl
from jax.experimental.pallas import tpu as pltpu
from jax.sharding import PartitionSpec as P


SEQ = 20
PART = 5
SIDE = 64
PAD = 8
TAIL = 64
LANES = 128


def score_kernel(
    slopes, q_ref, own_ref, other_ref, out_ref, top_ref,
    tail, similar, sums, squares, copies, part, part_late, half, half_late, best,
):
    rows, cols = out_ref.shape
    width = own_ref.shape[-1]
    features = own_ref.shape[1]
    depth = own_ref.shape[0] * features
    blocks = rows // LANES
    every = range(blocks + 1)
    first_col = lax.axis_index("dbcol") * cols
    total_cols = lax.axis_size("dbcol") * cols

    def rows_at(start):
        return pl.ds(pl.multiple_of(start, 8), 8)

    def tiles(start, count, unroll, body):
        def step(index, carry):
            body(start + index * 8)
            return carry

        lax.fori_loop(0, count, step, 0, unroll=unroll)

    own = own_ref[...].reshape(depth, width)
    other = other_ref[...].reshape(depth, width)

    tail[...] = jnp.zeros(tail.shape, jnp.float32)
    for at in range(features // 8):
        piece = q_ref[:, features:, at * TAIL : (at + 1) * TAIL].astype(jnp.float32)
        tail[:, at * 8 : at * 8 + 8, LANES - TAIL :] = piece

    here = lax.axis_index("qrow")
    order = []
    for by in range(4):
        for far in (0, 8):
            order.append(((here & 9) ^ far) | ((here - 2 * by) & 6))

    def multiply(right):
        total = None
        for core, piece in ((0, own), (1, other)):
            chosen = jnp.concatenate([right(which ^ core) for which in order], axis=0)
            product = lax.dot_general(
                piece, chosen, (((0,), (0,)), ((), ())), preferred_element_type=jnp.float32
            )
            total = product if total is None else total + product
        return total

    total = multiply(lambda which: q_ref[which, :features, :])
    for c in range(blocks):
        similar[c, PAD : PAD + width, :] = total[:, c * LANES : (c + 1) * LANES]
    similar[blocks, PAD : PAD + width, :] = multiply(
        lambda which: tail[which].astype(jnp.bfloat16)
    )

    def five(r):
        for c in every:
            x = [similar[c, pl.ds(r + d, 8), :] for d in range(5)]
            sums[c, rows_at(r), :] = (x[0] + x[1]) + (x[2] + x[3]) + x[4]
            x = [v * v for v in x]
            squares[c, rows_at(r), :] = (x[0] + x[1]) + (x[2] + x[3]) + x[4]

    tiles(0, (width + PAD) // 8, 49, five)

    lane = lax.broadcasted_iota(jnp.int32, (8, LANES), 1)
    sublane = lax.broadcasted_iota(jnp.int32, (8, LANES), 0)

    def rolled(values, by):
        turned = [pltpu.roll(v, by, axis=1) for v in values]
        return [jnp.where(lane < by, turned[c - 1], turned[c]) for c in range(len(values))]

    def normalise(r):
        col = sublane + (first_col + r - PAD - SIDE)
        low = jnp.maximum(col - 5, 0)
        high = jnp.minimum(col + 5, total_cols)
        inverse = 1.0 / jnp.maximum(high - low, 1).astype(jnp.float32)
        keep = jnp.where((col >= 0) & (col < total_cols), 1.0, 0.0)
        values = []
        for c in every:
            mean = (sums[c, pl.ds(r - 5, 8), :] + sums[c, rows_at(r), :]) * inverse
            square = (squares[c, pl.ds(r - 5, 8), :] + squares[c, rows_at(r), :]) * inverse
            var = square - mean * mean
            value = (similar[c, rows_at(r), :] - mean) * lax.rsqrt(jnp.maximum(var, 0.25)) * keep
            values.append(value.astype(jnp.bfloat16).astype(jnp.float32))
        for k in range(PART):
            for c, v in enumerate(rolled(values, k) if k else values):
                copies[k, c, rows_at(r), :] = v

    tiles(PAD, width // 8, 24, normalise)

    first = PAD + SIDE

    def one_slope(at, carry):
        slope = slopes[at]
        down = slope > 0
        start_half = jnp.where(down, first - 32, first)
        start_part = jnp.where(down, first - 48, first)

        def add_part(r):
            values = []
            for c in every:
                x = [copies[k, c, pl.ds(r - slope * k, 8), :] for k in range(PART)]
                values.append((x[0] + x[1]) + (x[2] + x[3]) + x[4])
            for c, v in enumerate(values):
                part[c, rows_at(r), :] = v
            for c, v in enumerate(rolled(values, PART)):
                part_late[c, rows_at(r), :] = v

        def add_half(r):
            values = [
                part[c, rows_at(r), :] + part_late[c, pl.ds(r - slope * PART, 8), :] for c in every
            ]
            for c, v in enumerate(values[:-1]):
                half[c, rows_at(r), :] = v
            for c, v in enumerate(rolled(values, 2 * PART)[:-1]):
                half_late[c, rows_at(r), :] = v

        def finish(r):
            for c in range(blocks):
                total = half[c, rows_at(r), :] + half_late[c, pl.ds(r - slope * 2 * PART, 8), :]
                best[c, rows_at(r - first), :] = jnp.maximum(
                    best[c, rows_at(r - first), :], total
                )

        tiles(start_part, (cols + 48) // 8, 38, add_part)
        tiles(start_half, (cols + 32) // 8, 36, add_half)
        tiles(first, cols // 8, 32, finish)
        return carry

    best[...] = jnp.full(best.shape, -jnp.inf, jnp.float32)
    lax.fori_loop(0, slopes.shape[0], one_slope, 0)

    scale = 1.0 / math.sqrt(SEQ)
    for c in range(blocks):
        scores = best[c] * scale
        out_ref[c * LANES : (c + 1) * LANES, :] = scores.T.astype(jnp.bfloat16)
        top_ref[:, c * LANES : (c + 1) * LANES] = jnp.max(scores, axis=0, keepdims=True)


def pack_kernel(query_ref, tail_ref, out_ref):
    features = query_ref.shape[0]
    tail = tail_ref[...].astype(jnp.float32)
    pieces = [tail[at : at + 8, :] for at in range(0, features, 8)]
    out_ref[:features, :] = query_ref[...]
    out_ref[features:, :] = jnp.concatenate(pieces, axis=1).astype(jnp.bfloat16)


def broadcast_to(x, peers):
    return jnp.broadcast_to(x[None], (peers,) + x.shape)


def local(query_desc, base_desc, slopes):
    rows, cols = query_desc.shape[0], base_desc.shape[0]
    across, down = lax.axis_size("dbcol"), lax.axis_size("qrow")
    query = query_desc.T
    base = base_desc.T
    depth = query.shape[0]

    right = [(i, i + 1) for i in range(across - 1)]
    before = lax.ppermute(base[:, cols - SIDE :], "dbcol", right)
    after = lax.ppermute(base[:, :SIDE], "dbcol", [(j, i) for i, j in right])
    tail = lax.ppermute(query[:, rows - TAIL :], "qrow", [(i, i + 1) for i in range(down - 1)])

    wide = jnp.concatenate([before, base, after], axis=1)
    def moved(x, target):
        return lax.ppermute(x, "qrow", [(i, target(i)) for i in range(down)])

    def y_later(by):
        return lambda i: (i & ~6) | ((i + 2 * by) & 6)

    pair = jnp.stack([wide, moved(wide, lambda i: i ^ 8)])
    own = jnp.stack([pair] + [moved(pair, y_later(by)) for by in range(1, 4)])
    own = own.reshape(down // 2, depth, wide.shape[1])
    other = moved(own, lambda i: i ^ 1)

    vmem = pl.BlockSpec(memory_space=pltpu.VMEM)
    block = pl.pallas_call(
        pack_kernel,
        out_shape=jax.ShapeDtypeStruct((depth + 8, rows), jnp.bfloat16),
        in_specs=[vmem, vmem],
        out_specs=vmem,
        name="pack",
    )(query, tail)
    query_all = lax.all_to_all(broadcast_to(block, across), "dbcol", 0, 0)

    def tall(lead):
        return pltpu.VMEM(lead + (cols + 2 * SIDE + 2 * PAD, LANES), jnp.float32)

    scores, top = pl.pallas_call(
        score_kernel,
        out_shape=(
            jax.ShapeDtypeStruct((rows, cols), jnp.bfloat16),
            jax.ShapeDtypeStruct((1, rows), jnp.float32),
        ),
        in_specs=[pl.BlockSpec(memory_space=pltpu.SMEM), vmem, vmem, vmem],
        out_specs=(vmem, vmem),
        scratch_shapes=[
            pltpu.VMEM((across, depth, LANES), jnp.float32),
            tall((rows // LANES + 1,)),
            tall((rows // LANES + 1,)),
            tall((rows // LANES + 1,)),
            tall((PART, rows // LANES + 1)),
            tall((rows // LANES + 1,)),
            tall((rows // LANES + 1,)),
            tall((rows // LANES,)),
            tall((rows // LANES,)),
            pltpu.VMEM((rows // LANES, cols, LANES), jnp.float32),
        ],
        name="score",
    )(
        slopes,
        query_all,
        own,
        other,
    )
    tops = lax.all_to_all(broadcast_to(top, across), "dbcol", 0, 0)
    return scores, jnp.max(tops[:, 0], axis=0)


def solution(mesh):
    placed = (P("qrow", "dbcol"), P("dbcol", "qrow"), P())
    return jax.shard_map(
        local,
        mesh=mesh,
        in_specs=placed,
        out_specs=(P("qrow", "dbcol"), P("qrow")),
        check_vma=False,
    )
```

```python
import math

import jax
import jax.numpy as jnp
from jax import lax
from jax.experimental import pallas as pl
from jax.experimental.pallas import tpu as pltpu
from jax.sharding import PartitionSpec as P


SEQ = 20
PART = 5
SIDE = 64
PAD = 8
TAIL = 64
LANES = 128


def score_kernel(
    slopes, q_ref, own_ref, other_ref, out_ref, top_ref,
    tail, similar, sums, squares, copies, part, part_late, half, half_late, best,
):
    rows, cols = out_ref.shape
    width = own_ref.shape[-1]
    features = own_ref.shape[1]
    depth = own_ref.shape[0] * features
    blocks = rows // LANES
    every = range(blocks + 1)
    first_col = lax.axis_index("dbcol") * cols
    total_cols = lax.axis_size("dbcol") * cols

    def rows_at(start):
        return pl.ds(pl.multiple_of(start, 8), 8)

    def tiles(start, count, unroll, body):
        def step(index, carry):
            body(start + index * 8)
            return carry

        lax.fori_loop(0, count, step, 0, unroll=unroll)

    own = own_ref[...].reshape(depth, width)
    other = other_ref[...].reshape(depth, width)

    tail[...] = jnp.zeros(tail.shape, jnp.float32)
    for at in range(features // 8):
        piece = q_ref[:, features:, at * TAIL : (at + 1) * TAIL].astype(jnp.float32)
        tail[:, at * 8 : at * 8 + 8, LANES - TAIL :] = piece

    here = lax.axis_index("qrow")
    order = []
    for by in range(4):
        for far in (0, 8):
            order.append(((here & 9) ^ far) | ((here - 2 * by) & 6))

    def multiply(right):
        total = None
        for core, piece in ((0, own), (1, other)):
            chosen = jnp.concatenate([right(which ^ core) for which in order], axis=0)
            product = lax.dot_general(
                piece, chosen, (((0,), (0,)), ((), ())), preferred_element_type=jnp.float32
            )
            total = product if total is None else total + product
        return total

    total = multiply(lambda which: q_ref[which, :features, :])
    for c in range(blocks):
        similar[c, PAD : PAD + width, :] = total[:, c * LANES : (c + 1) * LANES]
    similar[blocks, PAD : PAD + width, :] = multiply(
        lambda which: tail[which].astype(jnp.bfloat16)
    )

    def five(r):
        for c in every:
            x = [similar[c, pl.ds(r + d, 8), :] for d in range(5)]
            sums[c, rows_at(r), :] = (x[0] + x[1]) + (x[2] + x[3]) + x[4]
            x = [v * v for v in x]
            squares[c, rows_at(r), :] = (x[0] + x[1]) + (x[2] + x[3]) + x[4]

    tiles(0, (width + PAD) // 8, 49, five)

    lane = lax.broadcasted_iota(jnp.int32, (8, LANES), 1)
    sublane = lax.broadcasted_iota(jnp.int32, (8, LANES), 0)

    def rolled(values, by):
        turned = [pltpu.roll(v, by, axis=1) for v in values]
        return [jnp.where(lane < by, turned[c - 1], turned[c]) for c in range(len(values))]

    def normalise(r):
        col = sublane + (first_col + r - PAD - SIDE)
        low = jnp.maximum(col - 5, 0)
        high = jnp.minimum(col + 5, total_cols)
        inverse = 1.0 / jnp.maximum(high - low, 1).astype(jnp.float32)
        keep = jnp.where((col >= 0) & (col < total_cols), 1.0, 0.0)
        values = []
        for c in every:
            mean = (sums[c, pl.ds(r - 5, 8), :] + sums[c, rows_at(r), :]) * inverse
            square = (squares[c, pl.ds(r - 5, 8), :] + squares[c, rows_at(r), :]) * inverse
            var = square - mean * mean
            value = (similar[c, rows_at(r), :] - mean) * lax.rsqrt(jnp.maximum(var, 0.25)) * keep
            values.append(value.astype(jnp.bfloat16).astype(jnp.float32))
        for k in range(PART):
            for c, v in enumerate(rolled(values, k) if k else values):
                copies[k, c, rows_at(r), :] = v

    tiles(PAD, width // 8, 24, normalise)

    first = PAD + SIDE

    def one_slope(at, carry):
        slope = slopes[at]
        down = slope > 0
        start_half = jnp.where(down, first - 32, first)
        start_part = jnp.where(down, first - 48, first)

        def add_part(r):
            values = []
            for c in every:
                x = [copies[k, c, pl.ds(r - slope * k, 8), :] for k in range(PART)]
                values.append((x[0] + x[1]) + (x[2] + x[3]) + x[4])
            for c, v in enumerate(values):
                part[c, rows_at(r), :] = v
            for c, v in enumerate(rolled(values, PART)):
                part_late[c, rows_at(r), :] = v

        def add_half(r):
            values = [
                part[c, rows_at(r), :] + part_late[c, pl.ds(r - slope * PART, 8), :] for c in every
            ]
            for c, v in enumerate(values[:-1]):
                half[c, rows_at(r), :] = v
            for c, v in enumerate(rolled(values, 2 * PART)[:-1]):
                half_late[c, rows_at(r), :] = v

        def finish(r):
            for c in range(blocks):
                total = half[c, rows_at(r), :] + half_late[c, pl.ds(r - slope * 2 * PART, 8), :]
                best[c, rows_at(r - first), :] = jnp.maximum(
                    best[c, rows_at(r - first), :], total
                )

        tiles(start_part, (cols + 48) // 8, 38, add_part)
        tiles(start_half, (cols + 32) // 8, 36, add_half)
        tiles(first, cols // 8, 32, finish)
        return carry

    best[...] = jnp.full(best.shape, -jnp.inf, jnp.float32)
    lax.fori_loop(0, slopes.shape[0], one_slope, 0)

    scale = 1.0 / math.sqrt(SEQ)
    for c in range(blocks):
        scores = best[c] * scale
        out_ref[c * LANES : (c + 1) * LANES, :] = scores.T.astype(jnp.bfloat16)
        top_ref[:, c * LANES : (c + 1) * LANES] = jnp.max(scores, axis=0, keepdims=True)


def pack_kernel(query_ref, tail_ref, base_ref, before_ref, after_ref, out_ref, wide_ref):
    features, cols = base_ref.shape
    tail = tail_ref[...].astype(jnp.float32)
    pieces = [tail[at : at + 8, :] for at in range(0, features, 8)]
    packed = jnp.concatenate(pieces, axis=1).astype(jnp.bfloat16)
    query = query_ref[...]
    for peer in range(out_ref.shape[0]):
        out_ref[peer, :features, :] = query
        out_ref[peer, features:, :] = packed
    wide_ref[:, :SIDE] = before_ref[...]
    wide_ref[:, SIDE : SIDE + cols] = base_ref[...]
    wide_ref[:, SIDE + cols :] = after_ref[...]


def broadcast_to(x, peers):
    return jnp.broadcast_to(x[None], (peers,) + x.shape)


def local(query_desc, base_desc, slopes):
    rows, cols = query_desc.shape[0], base_desc.shape[0]
    across, down = lax.axis_size("dbcol"), lax.axis_size("qrow")
    query = query_desc.T
    base = base_desc.T
    depth = query.shape[0]

    right = [(i, i + 1) for i in range(across - 1)]
    before = lax.ppermute(base[:, cols - SIDE :], "dbcol", right)
    after = lax.ppermute(base[:, :SIDE], "dbcol", [(j, i) for i, j in right])
    tail = lax.ppermute(query[:, rows - TAIL :], "qrow", [(i, i + 1) for i in range(down - 1)])

    vmem = pl.BlockSpec(memory_space=pltpu.VMEM)
    blocks, wide = pl.pallas_call(
        pack_kernel,
        out_shape=(
            jax.ShapeDtypeStruct((across, depth + 8, rows), jnp.bfloat16),
            jax.ShapeDtypeStruct((depth, cols + 2 * SIDE), jnp.bfloat16),
        ),
        in_specs=[vmem] * 5,
        out_specs=(vmem, vmem),
        name="pack",
    )(query, tail, base, before, after)
    query_all = lax.all_to_all(blocks, "dbcol", 0, 0)

    def moved(x, target):
        return lax.ppermute(x, "qrow", [(i, target(i)) for i in range(down)])

    def y_later(by):
        return lambda i: (i & ~6) | ((i + 2 * by) & 6)

    pair = jnp.stack([wide, moved(wide, lambda i: i ^ 8)])
    own = jnp.stack([pair] + [moved(pair, y_later(by)) for by in range(1, 4)])
    own = own.reshape(down // 2, depth, wide.shape[1])
    other = moved(own, lambda i: i ^ 1)

    def tall(lead):
        return pltpu.VMEM(lead + (cols + 2 * SIDE + 2 * PAD, LANES), jnp.float32)

    scores, top = pl.pallas_call(
        score_kernel,
        out_shape=(
            jax.ShapeDtypeStruct((rows, cols), jnp.bfloat16),
            jax.ShapeDtypeStruct((1, rows), jnp.float32),
        ),
        in_specs=[pl.BlockSpec(memory_space=pltpu.SMEM), vmem, vmem, vmem],
        out_specs=(vmem, vmem),
        scratch_shapes=[
            pltpu.VMEM((across, depth, LANES), jnp.float32),
            tall((rows // LANES + 1,)),
            tall((rows // LANES + 1,)),
            tall((rows // LANES + 1,)),
            tall((PART, rows // LANES + 1)),
            tall((rows // LANES + 1,)),
            tall((rows // LANES + 1,)),
            tall((rows // LANES,)),
            tall((rows // LANES,)),
            pltpu.VMEM((rows // LANES, cols, LANES), jnp.float32),
        ],
        name="score",
    )(
        slopes,
        query_all,
        own,
        other,
    )
    tops = lax.all_to_all(broadcast_to(top, across), "dbcol", 0, 0)
    return scores, jnp.max(tops[:, 0], axis=0)


def solution(mesh):
    placed = (P("qrow", "dbcol"), P("dbcol", "qrow"), P())
    return jax.shard_map(
        local,
        mesh=mesh,
        in_specs=placed,
        out_specs=(P("qrow", "dbcol"), P("qrow")),
        check_vma=False,
    )
```

```python
import math

import jax
import jax.numpy as jnp
from jax import lax
from jax.experimental import pallas as pl
from jax.experimental.pallas import tpu as pltpu
from jax.sharding import PartitionSpec as P


SEQ = 20
PART = 5
SIDE = 64
PAD = 8
TAIL = 64
LANES = 128


def score_kernel(
    slopes, packed_ref, near_ref, far_ref, own_ref, other_ref, out_ref, top_ref,
    q_ref, sems, tail, similar, sums, squares, copies, part, part_late, half, half_late, best,
):
    rows, cols = out_ref.shape
    width = own_ref.shape[-1]
    features = own_ref.shape[1]
    depth = own_ref.shape[0] * features
    blocks = rows // LANES
    every = range(blocks + 1)
    first_col = lax.axis_index("dbcol") * cols
    total_cols = lax.axis_size("dbcol") * cols

    def rows_at(start):
        return pl.ds(pl.multiple_of(start, 8), 8)

    def tiles(start, count, unroll, body):
        def step(index, carry):
            body(start + index * 8)
            return carry

        lax.fori_loop(0, count, step, 0, unroll=unroll)

    own = own_ref[...].reshape(depth, width)
    other = other_ref[...].reshape(depth, width)

    side = lax.rem(lax.axis_index("dbcol"), 2)
    copies_in = [
        pltpu.make_async_copy(near_ref, q_ref.at[side], sems.at[0]),
        pltpu.make_async_copy(far_ref, q_ref.at[1 - side], sems.at[1]),
    ]
    for copy in copies_in:
        copy.start()
    for copy in copies_in:
        copy.wait()

    tail[...] = jnp.zeros(tail.shape, jnp.float32)
    for odd, source in ((side, packed_ref), (1 - side, q_ref.at[1 - side, :, features:])):
        for at in range(features // 8):
            piece = source[:, :, at * TAIL : (at + 1) * TAIL].astype(jnp.float32)
            tail[odd, :, at * 8 : at * 8 + 8, LANES - TAIL :] = piece

    here = lax.axis_index("qrow")
    core = lax.rem(here, 2)
    order = []
    for y in range(4):
        for far in (0, 4):
            order.append(((here // 8) * 4 ^ far) | y)

    def multiply(right):
        total = None
        for odd, piece in ((core, own), (1 - core, other)):
            chosen = jnp.concatenate([right(odd, which) for which in order], axis=0)
            product = lax.dot_general(
                piece, chosen, (((0,), (0,)), ((), ())), preferred_element_type=jnp.float32
            )
            total = product if total is None else total + product
        return total

    total = multiply(lambda odd, which: q_ref[odd, which, :features, :])
    for c in range(blocks):
        similar[c, PAD : PAD + width, :] = total[:, c * LANES : (c + 1) * LANES]
    similar[blocks, PAD : PAD + width, :] = multiply(
        lambda odd, which: tail[odd, which].astype(jnp.bfloat16)
    )

    def five(r):
        for c in every:
            x = [similar[c, pl.ds(r + d, 8), :] for d in range(5)]
            sums[c, rows_at(r), :] = (x[0] + x[1]) + (x[2] + x[3]) + x[4]
            x = [v * v for v in x]
            squares[c, rows_at(r), :] = (x[0] + x[1]) + (x[2] + x[3]) + x[4]

    tiles(0, (width + PAD) // 8, 49, five)

    lane = lax.broadcasted_iota(jnp.int32, (8, LANES), 1)
    sublane = lax.broadcasted_iota(jnp.int32, (8, LANES), 0)

    def rolled(values, by):
        turned = [pltpu.roll(v, by, axis=1) for v in values]
        return [jnp.where(lane < by, turned[c - 1], turned[c]) for c in range(len(values))]

    def normalise(r):
        col = sublane + (first_col + r - PAD - SIDE)
        low = jnp.maximum(col - 5, 0)
        high = jnp.minimum(col + 5, total_cols)
        inverse = 1.0 / jnp.maximum(high - low, 1).astype(jnp.float32)
        keep = jnp.where((col >= 0) & (col < total_cols), 1.0, 0.0)
        values = []
        for c in every:
            mean = (sums[c, pl.ds(r - 5, 8), :] + sums[c, rows_at(r), :]) * inverse
            square = (squares[c, pl.ds(r - 5, 8), :] + squares[c, rows_at(r), :]) * inverse
            var = square - mean * mean
            value = (similar[c, rows_at(r), :] - mean) * lax.rsqrt(jnp.maximum(var, 0.25)) * keep
            values.append(value.astype(jnp.bfloat16).astype(jnp.float32))
        for k in range(PART):
            for c, v in enumerate(rolled(values, k) if k else values):
                copies[k, c, rows_at(r), :] = v

    tiles(PAD, width // 8, 24, normalise)

    first = PAD + SIDE

    def one_slope(at, carry):
        slope = slopes[at]
        down = slope > 0
        start_half = jnp.where(down, first - 32, first)
        start_part = jnp.where(down, first - 48, first)

        def add_part(r):
            values = []
            for c in every:
                x = [copies[k, c, pl.ds(r - slope * k, 8), :] for k in range(PART)]
                values.append((x[0] + x[1]) + (x[2] + x[3]) + x[4])
            for c, v in enumerate(values):
                part[c, rows_at(r), :] = v
            for c, v in enumerate(rolled(values, PART)):
                part_late[c, rows_at(r), :] = v

        def add_half(r):
            values = [
                part[c, rows_at(r), :] + part_late[c, pl.ds(r - slope * PART, 8), :] for c in every
            ]
            for c, v in enumerate(values[:-1]):
                half[c, rows_at(r), :] = v
            for c, v in enumerate(rolled(values, 2 * PART)[:-1]):
                half_late[c, rows_at(r), :] = v

        def finish(r):
            for c in range(blocks):
                total = half[c, rows_at(r), :] + half_late[c, pl.ds(r - slope * 2 * PART, 8), :]
                best[c, rows_at(r - first), :] = jnp.maximum(
                    best[c, rows_at(r - first), :], total
                )

        tiles(start_part, (cols + 48) // 8, 38, add_part)
        tiles(start_half, (cols + 32) // 8, 36, add_half)
        tiles(first, cols // 8, 32, finish)
        return carry

    best[...] = jnp.full(best.shape, -jnp.inf, jnp.float32)
    lax.fori_loop(0, slopes.shape[0], one_slope, 0)

    scale = 1.0 / math.sqrt(SEQ)
    for c in range(blocks):
        scores = best[c] * scale
        out_ref[c * LANES : (c + 1) * LANES, :] = scores.T.astype(jnp.bfloat16)
        top_ref[:, c * LANES : (c + 1) * LANES] = jnp.max(scores, axis=0, keepdims=True)


def pack_kernel(query_ref, tail_ref, base_ref, before_ref, after_ref, out_ref, wide_ref):
    features, cols = base_ref.shape
    tail = tail_ref[...].astype(jnp.float32)
    pieces = [tail[at : at + 8, :] for at in range(0, features, 8)]
    out_ref[:features, :] = query_ref[...]
    out_ref[features:, :] = jnp.concatenate(pieces, axis=1).astype(jnp.bfloat16)
    wide_ref[:, :SIDE] = before_ref[...]
    wide_ref[:, SIDE : SIDE + cols] = base_ref[...]
    wide_ref[:, SIDE + cols :] = after_ref[...]


def broadcast_to(x, peers):
    return jnp.broadcast_to(x[None], (peers,) + x.shape)


def whole(query_desc, base_desc, slopes):
    rows, cols = query_desc.shape[0], base_desc.shape[0]
    across, down = lax.axis_size("dbcol"), lax.axis_size("qrow")
    query = query_desc.T
    base = base_desc.T
    depth = query.shape[0]

    right = [(i, i + 1) for i in range(across - 1)]
    before = lax.ppermute(base[:, cols - SIDE :], "dbcol", right)
    after = lax.ppermute(base[:, :SIDE], "dbcol", [(j, i) for i, j in right])
    tail = lax.ppermute(query[:, rows - TAIL :], "qrow", [(i, i + 1) for i in range(down - 1)])

    vmem = pl.BlockSpec(memory_space=pltpu.VMEM)
    hbm = pl.BlockSpec(memory_space=pl.ANY)
    block, wide = pl.pallas_call(
        pack_kernel,
        out_shape=(
            jax.ShapeDtypeStruct((depth + 8, rows), jnp.bfloat16),
            jax.ShapeDtypeStruct((depth, cols + 2 * SIDE), jnp.bfloat16),
        ),
        in_specs=[vmem] * 5,
        out_specs=(vmem, vmem),
        name="pack",
    )(query, tail, base, before, after)

    def moved(x, axis, bit):
        return lax.ppermute(x, axis, [(i, i ^ bit) for i in range(lax.axis_size(axis))])

    along_z = [[2 * z + x for z in range(across // 2)] for x in range(2)]
    along_y = [[8 * x + 2 * y + core for y in range(4)] for x in range(2) for core in range(2)]
    far = moved(wide, "qrow", 8)
    query_own = lax.all_to_all(
        broadcast_to(block, across // 2), "dbcol", 0, 0, axis_index_groups=along_z
    )
    packed = query_own[:, depth:, :]
    query_other = moved(query_own, "dbcol", 1)
    wide, far, query_own = lax.optimization_barrier((wide, far, query_own))
    own = lax.all_to_all(
        broadcast_to(jnp.stack([wide, far]), 4), "qrow", 0, 0, axis_index_groups=along_y
    )
    own = own.reshape(down // 2, depth, cols + 2 * SIDE)
    other = moved(own, "qrow", 1)

    def tall(lead):
        return pltpu.VMEM(lead + (cols + 2 * SIDE + 2 * PAD, LANES), jnp.float32)

    scores, top = pl.pallas_call(
        score_kernel,
        out_shape=(
            jax.ShapeDtypeStruct((rows, cols), jnp.bfloat16),
            jax.ShapeDtypeStruct((1, rows), jnp.float32),
        ),
        in_specs=[pl.BlockSpec(memory_space=pltpu.SMEM), vmem, hbm, hbm, vmem, vmem],
        out_specs=(vmem, vmem),
        scratch_shapes=[
            pltpu.VMEM((2, across // 2, depth + 8, rows), jnp.bfloat16),
            pltpu.SemaphoreType.DMA((2,)),
            pltpu.VMEM((2, across // 2, depth, LANES), jnp.float32),
            tall((rows // LANES + 1,)),
            tall((rows // LANES + 1,)),
            tall((rows // LANES + 1,)),
            tall((PART, rows // LANES + 1)),
            tall((rows // LANES + 1,)),
            tall((rows // LANES + 1,)),
            tall((rows // LANES,)),
            tall((rows // LANES,)),
            pltpu.VMEM((rows // LANES, cols, LANES), jnp.float32),
        ],
        name="score",
    )(
        slopes,
        packed,
        query_own,
        query_other,
        own,
        other,
    )
    tops = lax.all_to_all(broadcast_to(top, across), "dbcol", 0, 0)
    return scores, jnp.max(tops[:, 0], axis=0)


def solution(mesh):
    placed = (P("qrow", "dbcol"), P("dbcol", "qrow"), P())
    return jax.shard_map(
        whole,
        mesh=mesh,
        in_specs=placed,
        out_specs=(P("qrow", "dbcol"), P("qrow")),
        check_vma=False,
    )
```

```python
import math

import jax
import jax.numpy as jnp
from jax import lax
from jax.experimental import pallas as pl
from jax.experimental.pallas import tpu as pltpu
from jax.sharding import PartitionSpec as P


SEQ = 20
PART = 5
SIDE = 64
PAD = 8
TAIL = 64
LANES = 128


def score_kernel(
    slopes, q_ref, own_ref, other_ref, out_ref, top_ref,
    tail, similar, sums, squares, copies, part, part_late, half, half_late, best,
):
    rows, cols = out_ref.shape
    width = own_ref.shape[-1]
    features = own_ref.shape[1]
    depth = own_ref.shape[0] * features
    blocks = rows // LANES
    every = range(blocks + 1)
    first_col = lax.axis_index("dbcol") * cols
    total_cols = lax.axis_size("dbcol") * cols

    def rows_at(start):
        return pl.ds(pl.multiple_of(start, 8), 8)

    def tiles(start, count, unroll, body):
        def step(index, carry):
            body(start + index * 8)
            return carry

        lax.fori_loop(0, count, step, 0, unroll=unroll)

    own = own_ref[...].reshape(depth, width)
    other = other_ref[...].reshape(depth, width)

    tail[...] = jnp.zeros(tail.shape, jnp.float32)
    for at in range(features // 8):
        piece = q_ref[:, features:, at * TAIL : (at + 1) * TAIL].astype(jnp.float32)
        tail[:, at * 8 : at * 8 + 8, LANES - TAIL :] = piece

    here = lax.axis_index("qrow")
    order = []
    for by in range(4):
        for far in (0, 8):
            order.append(((here & 9) ^ far) | ((here - 2 * by) & 6))

    def multiply(right):
        total = None
        for core, piece in ((0, own), (1, other)):
            chosen = jnp.concatenate([right(which ^ core) for which in order], axis=0)
            product = lax.dot_general(
                piece, chosen, (((0,), (0,)), ((), ())), preferred_element_type=jnp.float32
            )
            total = product if total is None else total + product
        return total

    total = multiply(lambda which: q_ref[which, :features, :])
    for c in range(blocks):
        similar[c, PAD : PAD + width, :] = total[:, c * LANES : (c + 1) * LANES]
    similar[blocks, PAD : PAD + width, :] = multiply(
        lambda which: tail[which].astype(jnp.bfloat16)
    )

    def five(r):
        for c in every:
            x = [similar[c, pl.ds(r + d, 8), :] for d in range(5)]
            sums[c, rows_at(r), :] = (x[0] + x[1]) + (x[2] + x[3]) + x[4]
            x = [v * v for v in x]
            squares[c, rows_at(r), :] = (x[0] + x[1]) + (x[2] + x[3]) + x[4]

    tiles(0, (width + PAD) // 8, 49, five)

    lane = lax.broadcasted_iota(jnp.int32, (8, LANES), 1)
    sublane = lax.broadcasted_iota(jnp.int32, (8, LANES), 0)

    def rolled(values, by):
        turned = [pltpu.roll(v, by, axis=1) for v in values]
        return [jnp.where(lane < by, turned[c - 1], turned[c]) for c in range(len(values))]

    def normalise(r):
        col = sublane + (first_col + r - PAD - SIDE)
        low = jnp.maximum(col - 5, 0)
        high = jnp.minimum(col + 5, total_cols)
        inverse = 1.0 / jnp.maximum(high - low, 1).astype(jnp.float32)
        keep = jnp.where((col >= 0) & (col < total_cols), 1.0, 0.0)
        values = []
        for c in every:
            mean = (sums[c, pl.ds(r - 5, 8), :] + sums[c, rows_at(r), :]) * inverse
            square = (squares[c, pl.ds(r - 5, 8), :] + squares[c, rows_at(r), :]) * inverse
            var = square - mean * mean
            value = (similar[c, rows_at(r), :] - mean) * lax.rsqrt(jnp.maximum(var, 0.25)) * keep
            values.append(value.astype(jnp.bfloat16).astype(jnp.float32))
        for k in range(PART):
            for c, v in enumerate(rolled(values, k) if k else values):
                copies[k, c, rows_at(r), :] = v

    tiles(PAD, width // 8, 24, normalise)

    first = PAD + SIDE

    def one_slope(at, carry):
        slope = slopes[at]
        down = slope > 0
        start_half = jnp.where(down, first - 32, first)
        start_part = jnp.where(down, first - 48, first)

        def add_part(r):
            values = []
            for c in every:
                x = [copies[k, c, pl.ds(r - slope * k, 8), :] for k in range(PART)]
                values.append((x[0] + x[1]) + (x[2] + x[3]) + x[4])
            for c, v in enumerate(values):
                part[c, rows_at(r), :] = v
            for c, v in enumerate(rolled(values, PART)):
                part_late[c, rows_at(r), :] = v

        def add_half(r):
            values = [
                part[c, rows_at(r), :] + part_late[c, pl.ds(r - slope * PART, 8), :] for c in every
            ]
            for c, v in enumerate(values[:-1]):
                half[c, rows_at(r), :] = v
            for c, v in enumerate(rolled(values, 2 * PART)[:-1]):
                half_late[c, rows_at(r), :] = v

        def finish(r):
            for c in range(blocks):
                total = half[c, rows_at(r), :] + half_late[c, pl.ds(r - slope * 2 * PART, 8), :]
                best[c, rows_at(r - first), :] = jnp.maximum(
                    best[c, rows_at(r - first), :], total
                )

        tiles(start_part, (cols + 48) // 8, 38, add_part)
        tiles(start_half, (cols + 32) // 8, 36, add_half)
        tiles(first, cols // 8, 32, finish)
        return carry

    best[...] = jnp.full(best.shape, -jnp.inf, jnp.float32)
    lax.fori_loop(0, slopes.shape[0], one_slope, 0)

    scale = 1.0 / math.sqrt(SEQ)
    for c in range(blocks):
        scores = best[c] * scale
        out_ref[c * LANES : (c + 1) * LANES, :] = scores.T.astype(jnp.bfloat16)
        top_ref[:, c * LANES : (c + 1) * LANES] = jnp.max(scores, axis=0, keepdims=True)


def pack_kernel(query_ref, above_ref, base_ref, inner_ref, outer_ref, out_ref, wide_ref):
    features, cols = base_ref.shape
    rows = query_ref.shape[1]
    tail = above_ref[:, rows - TAIL :].astype(jnp.float32)
    pieces = [tail[at : at + 8, :] for at in range(0, features, 8)]
    packed = jnp.concatenate(pieces, axis=1).astype(jnp.bfloat16)
    query = query_ref[...]
    for peer in range(out_ref.shape[0]):
        out_ref[peer, :features, :] = query
        out_ref[peer, features:, :] = packed
    wide_ref[:, SIDE : SIDE + cols] = base_ref[...]
    odd = lax.rem(lax.axis_index("dbcol"), 2) == 1

    @pl.when(odd)
    def _():
        wide_ref[:, :SIDE] = inner_ref[:, cols - SIDE :]
        wide_ref[:, SIDE + cols :] = outer_ref[:, :SIDE]

    @pl.when(jnp.logical_not(odd))
    def _():
        wide_ref[:, :SIDE] = outer_ref[:, cols - SIDE :]
        wide_ref[:, SIDE + cols :] = inner_ref[:, :SIDE]


def kept(x):
    return pltpu.with_memory_space_constraint(x, pltpu.VMEM)


def broadcast_to(x, peers):
    return jnp.broadcast_to(x[None], (peers,) + x.shape)


def local(query_desc, base_desc, slopes):
    rows, cols = query_desc.shape[0], base_desc.shape[0]
    across, down = lax.axis_size("dbcol"), lax.axis_size("qrow")
    query = query_desc.T
    base = base_desc.T
    depth = query.shape[0]

    above = lax.ppermute(query, "qrow", [(i, i + 1) for i in range(down - 1)])
    inner = lax.ppermute(base, "dbcol", [(i, i ^ 1) for i in range(across)])
    outer = lax.ppermute(
        base, "dbcol", [(i, ((i + 1) ^ 1) - 1) for i in range(1, across - 1)]
    )

    vmem = pl.BlockSpec(memory_space=pltpu.VMEM)
    blocks, wide = pl.pallas_call(
        pack_kernel,
        out_shape=(
            jax.ShapeDtypeStruct((across, depth + 8, rows), jnp.bfloat16),
            jax.ShapeDtypeStruct((depth, cols + 2 * SIDE), jnp.bfloat16),
        ),
        in_specs=[vmem] * 5,
        out_specs=(vmem, vmem),
        name="pack",
    )(query, kept(above), base, kept(inner), kept(outer))
    query_all = lax.all_to_all(blocks, "dbcol", 0, 0)

    def moved(x, target):
        return lax.ppermute(x, "qrow", [(i, target(i)) for i in range(down)])

    def y_later(by):
        return lambda i: (i & ~6) | ((i + 2 * by) & 6)

    pair = jnp.stack([wide, moved(wide, lambda i: i ^ 8)])
    own = jnp.stack([pair] + [moved(pair, y_later(by)) for by in range(1, 4)])
    own = own.reshape(down // 2, depth, wide.shape[1])
    other = moved(own, lambda i: i ^ 1)

    def tall(lead):
        return pltpu.VMEM(lead + (cols + 2 * SIDE + 2 * PAD, LANES), jnp.float32)

    scores, top = pl.pallas_call(
        score_kernel,
        out_shape=(
            jax.ShapeDtypeStruct((rows, cols), jnp.bfloat16),
            jax.ShapeDtypeStruct((1, rows), jnp.float32),
        ),
        in_specs=[pl.BlockSpec(memory_space=pltpu.SMEM), vmem, vmem, vmem],
        out_specs=(vmem, vmem),
        scratch_shapes=[
            pltpu.VMEM((across, depth, LANES), jnp.float32),
            tall((rows // LANES + 1,)),
            tall((rows // LANES + 1,)),
            tall((rows // LANES + 1,)),
            tall((PART, rows // LANES + 1)),
            tall((rows // LANES + 1,)),
            tall((rows // LANES + 1,)),
            tall((rows // LANES,)),
            tall((rows // LANES,)),
            pltpu.VMEM((rows // LANES, cols, LANES), jnp.float32),
        ],
        name="score",
    )(
        slopes,
        kept(query_all),
        kept(own),
        kept(other),
    )
    tops = lax.all_to_all(broadcast_to(top, across), "dbcol", 0, 0)
    return scores, jnp.max(tops[:, 0], axis=0)


def solution(mesh):
    placed = (P("qrow", "dbcol"), P("dbcol", "qrow"), P())
    return jax.shard_map(
        local,
        mesh=mesh,
        in_specs=placed,
        out_specs=(P("qrow", "dbcol"), P("qrow")),
        check_vma=False,
    )
```

```python
import math

import jax
import jax.numpy as jnp
from jax import lax
from jax.experimental import pallas as pl
from jax.experimental.pallas import tpu as pltpu
from jax.sharding import PartitionSpec as P


SEQ = 20
PART = 5
SIDE = 64
PAD = 8
TAIL = 64
LANES = 128


def score_kernel(slopes, *refs):
    (own_ref, other_ref, out_ref, top_ref) = refs[-15:-11]
    (q_ref, tail, similar, sums, squares, copies, part, part_late, half, half_late, best) = refs[-11:]
    pieces = refs[:-15]
    rows, cols = out_ref.shape
    width = own_ref.shape[-1]
    features = own_ref.shape[1]
    depth = own_ref.shape[0] * features
    blocks = rows // LANES
    every = range(blocks + 1)
    first_col = lax.axis_index("dbcol") * cols
    total_cols = lax.axis_size("dbcol") * cols

    def rows_at(start):
        return pl.ds(pl.multiple_of(start, 8), 8)

    def tiles(start, count, unroll, body):
        def step(index, carry):
            body(start + index * 8)
            return carry

        lax.fori_loop(0, count, step, 0, unroll=unroll)

    own = own_ref[...].reshape(depth, width)
    other = other_ref[...].reshape(depth, width)

    side = lax.rem(lax.axis_index("dbcol"), 2)
    level, levels = lax.axis_index("dbcol") // 2, lax.axis_size("dbcol") // 2
    for at, piece in enumerate(pieces):
        step = (at + 1) // 2 if at % 2 else levels - at // 2
        source = lax.rem(level + levels - step, levels)
        last = at >= len(pieces) - 2
        for k in range(piece.shape[0]):
            way = 1 - side if k or (last and at % 2 == 0) else side
            q_ref[way, source] = piece[k]

    tail[...] = jnp.zeros(tail.shape, jnp.float32)
    for odd in range(2):
        for at in range(features // 8):
            piece = q_ref[odd, :, features:, at * TAIL : (at + 1) * TAIL].astype(jnp.float32)
            tail[odd, :, at * 8 : at * 8 + 8, LANES - TAIL :] = piece

    here = lax.axis_index("qrow")
    order = []
    for by in range(4):
        for far in (0, 8):
            order.append(((here & 9) ^ far) | ((here - 2 * by) & 6))

    def multiply(right):
        total = None
        for core, piece in ((0, own), (1, other)):
            chosen = jnp.concatenate([right(which ^ core) for which in order], axis=0)
            product = lax.dot_general(
                piece, chosen, (((0,), (0,)), ((), ())), preferred_element_type=jnp.float32
            )
            total = product if total is None else total + product
        return total

    total = multiply(lambda which: q_ref[which & 1, which >> 1, :features, :])
    for c in range(blocks):
        similar[c, PAD : PAD + width, :] = total[:, c * LANES : (c + 1) * LANES]
    similar[blocks, PAD : PAD + width, :] = multiply(
        lambda which: tail[which & 1, which >> 1].astype(jnp.bfloat16)
    )

    def five(r):
        for c in every:
            x = [similar[c, pl.ds(r + d, 8), :] for d in range(5)]
            sums[c, rows_at(r), :] = (x[0] + x[1]) + (x[2] + x[3]) + x[4]
            x = [v * v for v in x]
            squares[c, rows_at(r), :] = (x[0] + x[1]) + (x[2] + x[3]) + x[4]

    tiles(0, (width + PAD) // 8, 49, five)

    lane = lax.broadcasted_iota(jnp.int32, (8, LANES), 1)
    sublane = lax.broadcasted_iota(jnp.int32, (8, LANES), 0)

    def rolled(values, by):
        turned = [pltpu.roll(v, by, axis=1) for v in values]
        return [jnp.where(lane < by, turned[c - 1], turned[c]) for c in range(len(values))]

    def normalise(r):
        col = sublane + (first_col + r - PAD - SIDE)
        low = jnp.maximum(col - 5, 0)
        high = jnp.minimum(col + 5, total_cols)
        inverse = 1.0 / jnp.maximum(high - low, 1).astype(jnp.float32)
        keep = jnp.where((col >= 0) & (col < total_cols), 1.0, 0.0)
        values = []
        for c in every:
            mean = (sums[c, pl.ds(r - 5, 8), :] + sums[c, rows_at(r), :]) * inverse
            square = (squares[c, pl.ds(r - 5, 8), :] + squares[c, rows_at(r), :]) * inverse
            var = square - mean * mean
            value = (similar[c, rows_at(r), :] - mean) * lax.rsqrt(jnp.maximum(var, 0.25)) * keep
            values.append(value.astype(jnp.bfloat16).astype(jnp.float32))
        for k in range(PART):
            for c, v in enumerate(rolled(values, k) if k else values):
                copies[k, c, rows_at(r), :] = v

    tiles(PAD, width // 8, 24, normalise)

    first = PAD + SIDE

    def one_slope(at, carry):
        slope = slopes[at]
        down = slope > 0
        start_half = jnp.where(down, first - 32, first)
        start_part = jnp.where(down, first - 48, first)

        def add_part(r):
            values = []
            for c in every:
                x = [copies[k, c, pl.ds(r - slope * k, 8), :] for k in range(PART)]
                values.append((x[0] + x[1]) + (x[2] + x[3]) + x[4])
            for c, v in enumerate(values):
                part[c, rows_at(r), :] = v
            for c, v in enumerate(rolled(values, PART)):
                part_late[c, rows_at(r), :] = v

        def add_half(r):
            values = [
                part[c, rows_at(r), :] + part_late[c, pl.ds(r - slope * PART, 8), :] for c in every
            ]
            for c, v in enumerate(values[:-1]):
                half[c, rows_at(r), :] = v
            for c, v in enumerate(rolled(values, 2 * PART)[:-1]):
                half_late[c, rows_at(r), :] = v

        def finish(r):
            for c in range(blocks):
                total = half[c, rows_at(r), :] + half_late[c, pl.ds(r - slope * 2 * PART, 8), :]
                best[c, rows_at(r - first), :] = jnp.maximum(
                    best[c, rows_at(r - first), :], total
                )

        tiles(start_part, (cols + 48) // 8, 38, add_part)
        tiles(start_half, (cols + 32) // 8, 36, add_half)
        tiles(first, cols // 8, 32, finish)
        return carry

    best[...] = jnp.full(best.shape, -jnp.inf, jnp.float32)
    lax.fori_loop(0, slopes.shape[0], one_slope, 0)

    scale = 1.0 / math.sqrt(SEQ)
    for c in range(blocks):
        scores = best[c] * scale
        out_ref[c * LANES : (c + 1) * LANES, :] = scores.T.astype(jnp.bfloat16)
        most = jnp.max(scores, axis=0, keepdims=True)
        for peer in range(top_ref.shape[0]):
            top_ref[peer, :, c * LANES : (c + 1) * LANES] = most


def pack_kernel(query_ref, above_ref, base_ref, inner_ref, outer_ref, out_ref, wide_ref):
    features, cols = base_ref.shape
    rows = query_ref.shape[1]
    tail = above_ref[:, rows - TAIL :].astype(jnp.float32)
    pieces = [tail[at : at + 8, :] for at in range(0, features, 8)]
    packed = jnp.concatenate(pieces, axis=1).astype(jnp.bfloat16)
    out_ref[:features, :] = query_ref[...]
    out_ref[features:, :] = packed
    wide_ref[:, SIDE : SIDE + cols] = base_ref[...]
    odd = lax.rem(lax.axis_index("dbcol"), 2) == 1

    @pl.when(odd)
    def _():
        wide_ref[:, :SIDE] = inner_ref[:, cols - SIDE :]
        wide_ref[:, SIDE + cols :] = outer_ref[:, :SIDE]

    @pl.when(jnp.logical_not(odd))
    def _():
        wide_ref[:, :SIDE] = outer_ref[:, cols - SIDE :]
        wide_ref[:, SIDE + cols :] = inner_ref[:, :SIDE]


def kept(x):
    return pltpu.with_memory_space_constraint(x, pltpu.VMEM)


def local(query_desc, base_desc, slopes):
    rows, cols = query_desc.shape[0], base_desc.shape[0]
    across, down = lax.axis_size("dbcol"), lax.axis_size("qrow")
    query = query_desc.T
    base = base_desc.T
    depth = query.shape[0]

    above = lax.ppermute(query, "qrow", [(i, i + 1) for i in range(down - 1)])
    inner = lax.ppermute(base, "dbcol", [(i, i ^ 1) for i in range(across)])
    outer = lax.ppermute(
        base, "dbcol", [(i, ((i + 1) ^ 1) - 1) for i in range(1, across - 1)]
    )

    vmem = pl.BlockSpec(memory_space=pltpu.VMEM)
    block, wide = pl.pallas_call(
        pack_kernel,
        out_shape=(
            jax.ShapeDtypeStruct((depth + 8, rows), jnp.bfloat16),
            jax.ShapeDtypeStruct((depth, cols + 2 * SIDE), jnp.bfloat16),
        ),
        in_specs=[vmem] * 5,
        out_specs=(vmem, vmem),
        name="pack",
    )(query, kept(above), base, kept(inner), kept(outer))

    def along_z(x, by):
        return lax.ppermute(x, "dbcol", [(i, (i + 2 * by) % across) for i in range(across)])

    mate = lax.ppermute(block, "dbcol", [(i, i ^ 1) for i in range(across)])
    hops = across // 4
    ups = downs = jnp.stack([block, mate])
    pieces = [ups]
    for hop in range(1, hops):
        ups, downs = along_z(ups, 1), along_z(downs, -1)
        pieces += [ups, downs]
    pieces += [along_z(ups[:1], 1), along_z(downs[1:], -1)]

    def moved(x, target):
        return lax.ppermute(x, "qrow", [(i, target(i)) for i in range(down)])

    def y_later(by):
        return lambda i: (i & ~6) | ((i + 2 * by) & 6)

    pair = jnp.stack([wide, moved(wide, lambda i: i ^ 8)])
    own = jnp.stack([pair] + [moved(pair, y_later(by)) for by in range(1, 4)])
    own = own.reshape(down // 2, depth, wide.shape[1])
    other = moved(own, lambda i: i ^ 1)

    def tall(lead):
        return pltpu.VMEM(lead + (cols + 2 * SIDE + 2 * PAD, LANES), jnp.float32)

    scores, top = pl.pallas_call(
        score_kernel,
        out_shape=(
            jax.ShapeDtypeStruct((rows, cols), jnp.bfloat16),
            jax.ShapeDtypeStruct((across, 1, rows), jnp.float32),
        ),
        in_specs=[pl.BlockSpec(memory_space=pltpu.SMEM)] + [vmem] * (len(pieces) + 2),
        out_specs=(vmem, vmem),
        scratch_shapes=[
            pltpu.VMEM((2, across // 2, depth + 8, rows), jnp.bfloat16),
            pltpu.VMEM((2, across // 2, depth, LANES), jnp.float32),
            tall((rows // LANES + 1,)),
            tall((rows // LANES + 1,)),
            tall((rows // LANES + 1,)),
            tall((PART, rows // LANES + 1)),
            tall((rows // LANES + 1,)),
            tall((rows // LANES + 1,)),
            tall((rows // LANES,)),
            tall((rows // LANES,)),
            pltpu.VMEM((rows // LANES, cols, LANES), jnp.float32),
        ],
        name="score",
    )(
        slopes,
        *map(kept, pieces),
        kept(own),
        kept(other),
    )
    tops = lax.all_to_all(top, "dbcol", 0, 0)
    return scores, jnp.max(tops[:, 0], axis=0)


def solution(mesh):
    placed = (P("qrow", "dbcol"), P("dbcol", "qrow"), P())
    return jax.shard_map(
        local,
        mesh=mesh,
        in_specs=placed,
        out_specs=(P("qrow", "dbcol"), P("qrow")),
        check_vma=False,
    )
```

```python
import math

import jax
import jax.numpy as jnp
from jax import lax
from jax.experimental import pallas as pl
from jax.experimental.pallas import tpu as pltpu
from jax.sharding import PartitionSpec as P


SEQ = 20
PART = 5
SIDE = 64
PAD = 8
TAIL = 128
LANES = 128


def score_kernel(
    slopes, q_ref, tail_ref, own_ref, other_ref, out_ref, top_ref,
    similar, sums, squares, copies, part, part_late, half, half_late, best,
):
    rows, cols = out_ref.shape
    width = own_ref.shape[-1]
    features = own_ref.shape[1]
    depth = own_ref.shape[0] * features
    blocks = rows // LANES
    every = range(blocks + 1)
    parity = lax.rem(lax.axis_index("qrow"), 2)
    first_col = lax.axis_index("dbcol") * cols
    total_cols = lax.axis_size("dbcol") * cols

    def rows_at(start):
        return pl.ds(pl.multiple_of(start, 8), 8)

    def tiles(start, count, unroll, body):
        def step(index, carry):
            body(start + index * 8)
            return carry

        lax.fori_loop(0, count, step, 0, unroll=unroll)

    own = own_ref[...].reshape(depth, width)
    other = other_ref[...].reshape(depth, width)
    for ref, low, count, block in ((q_ref, 0, rows, 0), (tail_ref, 0, TAIL, blocks)):
        total = None
        for which, piece in ((parity, own), (1 - parity, other)):
            right = ref[:, which, :features, low : low + count].reshape(depth, count)
            product = lax.dot_general(
                piece, right, (((0,), (0,)), ((), ())), preferred_element_type=jnp.float32
            )
            total = product if total is None else total + product
        for c in range(count // LANES):
            similar[block + c, PAD : PAD + width, :] = total[:, c * LANES : (c + 1) * LANES]

    def five(r):
        for c in every:
            x = [similar[c, pl.ds(r + d, 8), :] for d in range(5)]
            sums[c, rows_at(r), :] = (x[0] + x[1]) + (x[2] + x[3]) + x[4]
            x = [v * v for v in x]
            squares[c, rows_at(r), :] = (x[0] + x[1]) + (x[2] + x[3]) + x[4]

    tiles(0, (width + PAD) // 8, 49, five)

    lane = lax.broadcasted_iota(jnp.int32, (8, LANES), 1)
    sublane = lax.broadcasted_iota(jnp.int32, (8, LANES), 0)

    def rolled(values, by):
        turned = [pltpu.roll(v, by, axis=1) for v in values]
        return [jnp.where(lane < by, turned[c - 1], turned[c]) for c in range(len(values))]

    def normalise(r):
        col = sublane + (first_col + r - PAD - SIDE)
        low = jnp.maximum(col - 5, 0)
        high = jnp.minimum(col + 5, total_cols)
        inverse = 1.0 / jnp.maximum(high - low, 1).astype(jnp.float32)
        keep = jnp.where((col >= 0) & (col < total_cols), 1.0, 0.0)
        values = []
        for c in every:
            mean = (sums[c, pl.ds(r - 5, 8), :] + sums[c, rows_at(r), :]) * inverse
            square = (squares[c, pl.ds(r - 5, 8), :] + squares[c, rows_at(r), :]) * inverse
            var = square - mean * mean
            value = (similar[c, rows_at(r), :] - mean) * lax.rsqrt(jnp.maximum(var, 0.25)) * keep
            values.append(value.astype(jnp.bfloat16).astype(jnp.float32))
        for k in range(PART):
            for c, v in enumerate(rolled(values, k) if k else values):
                copies[k, c, rows_at(r), :] = v

    tiles(PAD, width // 8, 48, normalise)

    first = PAD + SIDE

    def one_slope(at, carry):
        slope = slopes[at]
        down = slope > 0
        start_half = jnp.where(down, first - 32, first)
        start_part = jnp.where(down, first - 48, first)

        def add_part(r):
            values = []
            for c in every:
                x = [copies[k, c, pl.ds(r - slope * k, 8), :] for k in range(PART)]
                values.append((x[0] + x[1]) + (x[2] + x[3]) + x[4])
            for c, v in enumerate(values):
                part[c, rows_at(r), :] = v
            for c, v in enumerate(rolled(values, PART)):
                part_late[c, rows_at(r), :] = v

        def add_half(r):
            values = [
                part[c, rows_at(r), :] + part_late[c, pl.ds(r - slope * PART, 8), :] for c in every
            ]
            for c, v in enumerate(values[:-1]):
                half[c, rows_at(r), :] = v
            for c, v in enumerate(rolled(values, 2 * PART)[:-1]):
                half_late[c, rows_at(r), :] = v

        def finish(r):
            for c in range(blocks):
                total = half[c, rows_at(r), :] + half_late[c, pl.ds(r - slope * 2 * PART, 8), :]
                best[c, rows_at(r - first), :] = jnp.maximum(
                    best[c, rows_at(r - first), :], total
                )

        tiles(start_part, (cols + 48) // 8, 38, add_part)
        tiles(start_half, (cols + 32) // 8, 36, add_half)
        tiles(first, cols // 8, 32, finish)
        return carry

    best[...] = jnp.full(best.shape, -jnp.inf, jnp.float32)
    lax.fori_loop(0, slopes.shape[0], one_slope, 0)

    scale = 1.0 / math.sqrt(SEQ)
    for c in range(blocks):
        scores = best[c] * scale
        out_ref[c * LANES : (c + 1) * LANES, :] = scores.T.astype(jnp.bfloat16)
        most = jnp.max(scores, axis=0, keepdims=True)
        for peer in range(top_ref.shape[0]):
            top_ref[peer, :, c * LANES : (c + 1) * LANES] = most


def pack_kernel(query_ref, base_ref, out_ref):
    features, cols = base_ref.shape
    base = base_ref[...].astype(jnp.float32)

    def packed(low):
        pieces = [base[at : at + 8, low : low + SIDE] for at in range(0, features, 8)]
        return jnp.concatenate(pieces, axis=1).astype(jnp.bfloat16)

    low, high = packed(0), packed(cols - SIDE)
    query = query_ref[...]
    for at, edge in enumerate((low, high)):
        out_ref[at, :features, :] = query
        out_ref[at, features:, :] = edge


def widen_kernel(all_ref, base_ref, out_ref):
    features, _ = base_ref.shape
    here = lax.axis_index("dbcol")
    last = lax.axis_size("dbcol") - 1

    def unpacked(peer, inside):
        edge = all_ref[jnp.clip(peer, 0, last), features:, :].astype(jnp.float32)
        edge = jnp.where(inside, edge, 0.0)
        pieces = [edge[:, low : low + SIDE] for low in range(0, edge.shape[1], SIDE)]
        return jnp.concatenate(pieces, axis=0)

    base = base_ref[...].astype(jnp.float32)
    wide = [unpacked(here - 1, here > 0), base, unpacked(here + 1, here < last)]
    out_ref[...] = jnp.concatenate(wide, axis=1).astype(jnp.bfloat16)


def kept(x):
    return pltpu.with_memory_space_constraint(x, pltpu.VMEM)


def broadcast_to(x, peers):
    return jnp.broadcast_to(x[None], (peers,) + x.shape)


def whole(query_desc, base_desc, slopes):
    rows, cols = query_desc.shape[0], base_desc.shape[0]
    across, down = lax.axis_size("dbcol"), lax.axis_size("qrow")
    query = query_desc.T
    base = base_desc.T
    depth = query.shape[0]

    vmem = pl.BlockSpec(memory_space=pltpu.VMEM)
    pair = pl.pallas_call(
        pack_kernel,
        out_shape=jax.ShapeDtypeStruct((2, depth + 8, rows), jnp.bfloat16),
        in_specs=[vmem, vmem],
        out_specs=vmem,
        name="pack",
    )(query, base)
    ahead = (jnp.arange(across) > lax.axis_index("dbcol"))[:, None, None]
    blocks = jnp.where(ahead, pair[1][None], pair[0][None])
    query_all = lax.all_to_all(blocks, "dbcol", 0, 0)
    tail = lax.ppermute(
        query_all[:, :depth, rows - TAIL :], "qrow", [(i, i + 1) for i in range(down - 1)]
    )
    wide = pl.pallas_call(
        widen_kernel,
        out_shape=jax.ShapeDtypeStruct((depth, cols + 2 * SIDE), jnp.bfloat16),
        in_specs=[vmem, vmem],
        out_specs=vmem,
        name="widen",
    )(kept(query_all), base)
    same_core = [[2 * k + core for k in range(down // 2)] for core in range(2)]
    own = lax.all_to_all(broadcast_to(wide, down // 2), "qrow", 0, 0, axis_index_groups=same_core)
    other = lax.ppermute(own, "qrow", [(i, i ^ 1) for i in range(down)])

    def tall(lead):
        return pltpu.VMEM(lead + (cols + 2 * SIDE + 2 * PAD, LANES), jnp.float32)

    scores, top = pl.pallas_call(
        score_kernel,
        out_shape=(
            jax.ShapeDtypeStruct((rows, cols), jnp.bfloat16),
            jax.ShapeDtypeStruct((across, 1, rows), jnp.float32),
        ),
        in_specs=[pl.BlockSpec(memory_space=pltpu.SMEM), vmem, vmem, vmem, vmem],
        out_specs=(vmem, vmem),
        scratch_shapes=[
            tall((rows // LANES + 1,)),
            tall((rows // LANES + 1,)),
            tall((rows // LANES + 1,)),
            tall((PART, rows // LANES + 1)),
            tall((rows // LANES + 1,)),
            tall((rows // LANES + 1,)),
            tall((rows // LANES,)),
            tall((rows // LANES,)),
            pltpu.VMEM((rows // LANES, cols, LANES), jnp.float32),
        ],
        name="score",
    )(
        slopes,
        kept(query_all.reshape(across // 2, 2, depth + 8, rows)),
        kept(tail.reshape(across // 2, 2, depth, TAIL)),
        kept(own),
        kept(other),
    )
    tops = lax.all_to_all(top, "dbcol", 0, 0)
    return scores, jnp.max(tops[:, 0], axis=0)


def solution(mesh):
    placed = (P("qrow", "dbcol"), P("dbcol", "qrow"), P())
    return jax.shard_map(
        whole,
        mesh=mesh,
        in_specs=placed,
        out_specs=(P("qrow", "dbcol"), P("qrow")),
        check_vma=False,
    )
```

```python
import math

import jax
import jax.numpy as jnp
from jax import lax
from jax.experimental import pallas as pl
from jax.experimental.pallas import tpu as pltpu
from jax.sharding import PartitionSpec as P


SEQ = 20
PART = 5
SIDE = 64
PAD = 8
TAIL = 64
LANES = 128


def score_kernel(
    slopes, q_ref, own_ref, other_ref, out_ref, top_ref,
    tail, similar, sums, squares, copies, part, part_late, half, half_late, best,
):
    rows, cols = out_ref.shape
    width = own_ref.shape[-1]
    features = own_ref.shape[1]
    depth = own_ref.shape[0] * features
    blocks = rows // LANES
    every = range(blocks + 1)
    first_col = lax.axis_index("dbcol") * cols
    total_cols = lax.axis_size("dbcol") * cols

    def rows_at(start):
        return pl.ds(pl.multiple_of(start, 8), 8)

    def tiles(start, count, unroll, body):
        def step(index, carry):
            body(start + index * 8)
            return carry

        lax.fori_loop(0, count, step, 0, unroll=unroll)

    own = own_ref[...].reshape(depth, width)
    other = other_ref[...].reshape(depth, width)

    tail[...] = jnp.zeros(tail.shape, jnp.float32)
    for at in range(features // 8):
        piece = q_ref[:, features:, at * TAIL : (at + 1) * TAIL].astype(jnp.float32)
        tail[:, at * 8 : at * 8 + 8, LANES - TAIL :] = piece

    here = lax.axis_index("qrow")
    order = []
    for by in range(4):
        for far in (0, 8):
            order.append(((here & 9) ^ far) | ((here - 2 * by) & 6))

    def multiply(right):
        total = None
        for core, piece in ((0, own), (1, other)):
            chosen = jnp.concatenate([right(which ^ core) for which in order], axis=0)
            product = lax.dot_general(
                piece, chosen, (((0,), (0,)), ((), ())), preferred_element_type=jnp.float32
            )
            total = product if total is None else total + product
        return total

    total = multiply(lambda which: q_ref[which, :features, :])
    for c in range(blocks):
        similar[c, PAD : PAD + width, :] = total[:, c * LANES : (c + 1) * LANES]
    similar[blocks, PAD : PAD + width, :] = multiply(
        lambda which: tail[which].astype(jnp.bfloat16)
    )

    def five(r):
        for c in every:
            x = [similar[c, pl.ds(r + d, 8), :] for d in range(5)]
            sums[c, rows_at(r), :] = (x[0] + x[1]) + (x[2] + x[3]) + x[4]
            x = [v * v for v in x]
            squares[c, rows_at(r), :] = (x[0] + x[1]) + (x[2] + x[3]) + x[4]

    tiles(0, (width + PAD) // 8, 49, five)

    lane = lax.broadcasted_iota(jnp.int32, (8, LANES), 1)
    sublane = lax.broadcasted_iota(jnp.int32, (8, LANES), 0)

    def rolled(values, by):
        turned = [pltpu.roll(v, by, axis=1) for v in values]
        return [jnp.where(lane < by, turned[c - 1], turned[c]) for c in range(len(values))]

    def normalise(r):
        col = sublane + (first_col + r - PAD - SIDE)
        low = jnp.maximum(col - 5, 0)
        high = jnp.minimum(col + 5, total_cols)
        inverse = 1.0 / jnp.maximum(high - low, 1).astype(jnp.float32)
        keep = jnp.where((col >= 0) & (col < total_cols), 1.0, 0.0)
        values = []
        for c in every:
            mean = (sums[c, pl.ds(r - 5, 8), :] + sums[c, rows_at(r), :]) * inverse
            square = (squares[c, pl.ds(r - 5, 8), :] + squares[c, rows_at(r), :]) * inverse
            var = square - mean * mean
            value = (similar[c, rows_at(r), :] - mean) * lax.rsqrt(jnp.maximum(var, 0.25)) * keep
            values.append(value.astype(jnp.bfloat16).astype(jnp.float32))
        for k in range(PART):
            for c, v in enumerate(rolled(values, k) if k else values):
                copies[k, c, rows_at(r), :] = v

    tiles(PAD, width // 8, 48, normalise)

    first = PAD + SIDE

    def one_slope(at, carry):
        slope = slopes[at]
        down = slope > 0
        start_half = jnp.where(down, first - 32, first)
        start_part = jnp.where(down, first - 48, first)

        def add_part(r):
            values = []
            for c in every:
                x = [copies[k, c, pl.ds(r - slope * k, 8), :] for k in range(PART)]
                values.append((x[0] + x[1]) + (x[2] + x[3]) + x[4])
            for c, v in enumerate(values):
                part[c, rows_at(r), :] = v
            for c, v in enumerate(rolled(values, PART)):
                part_late[c, rows_at(r), :] = v

        def add_half(r):
            values = [
                part[c, rows_at(r), :] + part_late[c, pl.ds(r - slope * PART, 8), :] for c in every
            ]
            for c, v in enumerate(values[:-1]):
                half[c, rows_at(r), :] = v
            for c, v in enumerate(rolled(values, 2 * PART)[:-1]):
                half_late[c, rows_at(r), :] = v

        def finish(r):
            for c in range(blocks):
                total = half[c, rows_at(r), :] + half_late[c, pl.ds(r - slope * 2 * PART, 8), :]
                best[c, rows_at(r - first), :] = jnp.maximum(
                    best[c, rows_at(r - first), :], total
                )

        tiles(start_part, (cols + 48) // 8, 38, add_part)
        tiles(start_half, (cols + 32) // 8, 36, add_half)
        tiles(first, cols // 8, 32, finish)
        return carry

    best[...] = jnp.full(best.shape, -jnp.inf, jnp.float32)
    lax.fori_loop(0, slopes.shape[0], one_slope, 0)

    scale = 1.0 / math.sqrt(SEQ)
    for c in range(blocks):
        scores = best[c] * scale
        out_ref[c * LANES : (c + 1) * LANES, :] = scores.T.astype(jnp.bfloat16)
        top_ref[:, c * LANES : (c + 1) * LANES] = jnp.max(scores, axis=0, keepdims=True)


def pack_kernel(query_ref, above_ref, out_ref):
    features, rows = query_ref.shape
    tail = above_ref[:, rows - TAIL :].astype(jnp.float32)
    pieces = [tail[at : at + 8, :] for at in range(0, features, 8)]
    packed = jnp.concatenate(pieces, axis=1).astype(jnp.bfloat16)
    query = query_ref[...]
    for peer in range(out_ref.shape[0]):
        out_ref[peer, :features, :] = query
        out_ref[peer, features:, :] = packed


def widen_kernel(base_ref, inner_ref, outer_ref, wide_ref):
    cols = base_ref.shape[1]
    wide_ref[:, SIDE : SIDE + cols] = base_ref[...]
    odd = lax.rem(lax.axis_index("dbcol"), 2) == 1

    @pl.when(odd)
    def _():
        wide_ref[:, :SIDE] = inner_ref[:, cols - SIDE :]
        wide_ref[:, SIDE + cols :] = outer_ref[:, :SIDE]

    @pl.when(jnp.logical_not(odd))
    def _():
        wide_ref[:, :SIDE] = outer_ref[:, cols - SIDE :]
        wide_ref[:, SIDE + cols :] = inner_ref[:, :SIDE]


def kept(x):
    return pltpu.with_memory_space_constraint(x, pltpu.VMEM)


def broadcast_to(x, peers):
    return jnp.broadcast_to(x[None], (peers,) + x.shape)


def whole(query_desc, base_desc, slopes):
    rows, cols = query_desc.shape[0], base_desc.shape[0]
    across, down = lax.axis_size("dbcol"), lax.axis_size("qrow")
    query = query_desc.T
    base = base_desc.T
    depth = query.shape[0]

    above = lax.ppermute(query, "qrow", [(i, i + 1) for i in range(down - 1)])
    inner = lax.ppermute(base, "dbcol", [(i, i ^ 1) for i in range(across)])
    outer = lax.ppermute(
        base, "dbcol", [(i, ((i + 1) ^ 1) - 1) for i in range(1, across - 1)]
    )

    vmem = pl.BlockSpec(memory_space=pltpu.VMEM)
    blocks = pl.pallas_call(
        pack_kernel,
        out_shape=jax.ShapeDtypeStruct((across, depth + 8, rows), jnp.bfloat16),
        in_specs=[vmem] * 2,
        out_specs=vmem,
        name="pack",
    )(query, kept(above))
    wide = pl.pallas_call(
        widen_kernel,
        out_shape=jax.ShapeDtypeStruct((depth, cols + 2 * SIDE), jnp.bfloat16),
        in_specs=[vmem] * 3,
        out_specs=vmem,
        name="widen",
    )(base, kept(inner), kept(outer))
    query_all = lax.all_to_all(blocks, "dbcol", 0, 0)

    def moved(x, target):
        return lax.ppermute(x, "qrow", [(i, target(i)) for i in range(down)])

    def y_later(by):
        return lambda i: (i & ~6) | ((i + 2 * by) & 6)

    pair = jnp.stack([wide, moved(wide, lambda i: i ^ 8)])
    own = jnp.stack([pair] + [moved(pair, y_later(by)) for by in range(1, 4)])
    own = own.reshape(down // 2, depth, wide.shape[1])
    other = moved(own, lambda i: i ^ 1)

    def tall(lead):
        return pltpu.VMEM(lead + (cols + 2 * SIDE + 2 * PAD, LANES), jnp.float32)

    scores, top = pl.pallas_call(
        score_kernel,
        out_shape=(
            jax.ShapeDtypeStruct((rows, cols), jnp.bfloat16),
            jax.ShapeDtypeStruct((1, rows), jnp.float32),
        ),
        in_specs=[pl.BlockSpec(memory_space=pltpu.SMEM), vmem, vmem, vmem],
        out_specs=(vmem, vmem),
        scratch_shapes=[
            pltpu.VMEM((across, depth, LANES), jnp.float32),
            tall((rows // LANES + 1,)),
            tall((rows // LANES + 1,)),
            tall((rows // LANES + 1,)),
            tall((PART, rows // LANES + 1)),
            tall((rows // LANES + 1,)),
            tall((rows // LANES + 1,)),
            tall((rows // LANES,)),
            tall((rows // LANES,)),
            pltpu.VMEM((rows // LANES, cols, LANES), jnp.float32),
        ],
        name="score",
    )(
        slopes,
        kept(query_all),
        kept(own),
        kept(other),
    )
    tops = lax.all_to_all(broadcast_to(top, across), "dbcol", 0, 0)
    return scores, jnp.max(tops[:, 0], axis=0)


def solution(mesh):
    placed = (P("qrow", "dbcol"), P("dbcol", "qrow"), P())
    return jax.shard_map(
        whole,
        mesh=mesh,
        in_specs=placed,
        out_specs=(P("qrow", "dbcol"), P("qrow")),
        check_vma=False,
    )
```
